512 devices in a mesh: fsdp: 64 (over y_lo, z, core), expert: 8 (over y_hi, x).
Axes of the slice: x: 4, y: 4 (y_hi: 2, y_lo: 2; y = y_hi * 2 + y_lo), z: 16, core: 2. Of those that a mesh axis runs over, the one named last changes fastest.
Arguments:
- tokens: bfloat16 [8192, 5120], P('expert', 'fsdp'), may hold values from -6 to 6
- out_grad: bfloat16 [8192, 5120], P('expert', 'fsdp'), may hold values from -6 to 6
- slot_rows: int32 [8, 8, 24], P('expert'), may hold values from 0 to 1023, as said below
- expert_counts: int32 [8, 8], P('expert'), may hold values from 1 to 24, as said below
- route_prob: float32 [8, 192], P('expert'), may hold values from 0.05 to 0.9
- w_gate: bfloat16 [8, 5120, 1536], P('expert', 'fsdp'), may hold values from -0.078125 to 0.078125
- w_up: bfloat16 [8, 5120, 1536], P('expert', 'fsdp'), may hold values from -0.078125 to 0.078125
- w_down: bfloat16 [8, 5120, 1536], P('expert', 'fsdp'), may hold values from -0.15625 to 0.15625
Outputs:
- token_grad: bfloat16 [8192, 5120], P('expert', 'fsdp')
- gate_grad: float32 [8, 5120, 1536], P('expert', 'fsdp')
- up_grad: float32 [8, 5120, 1536], P('expert', 'fsdp')
- down_grad: float32 [8, 5120, 1536], P('expert', 'fsdp')
- prob_grad: float32 [8, 192], P('expert', 'fsdp')
The draws below stay inside these ranges and needn't reach their ends.
Inputs may be any that keep to these rules, and one draw needn't show every extreme that they name: `slot_rows`: for each token group and expert the 24 listed rows are distinct. `expert_counts`: in every draw one expert has all 24 slots live from every token group.
All inputs are finite; a program needn't handle non-finite values.
Results may differ from the reference program's by a relative error of at most 0.0055.
Values may be sent and summed in bfloat16 or wider, within the bound.
A program may use at most 64 MiB of HBM per device.

```python
import math
import jax
import jax.numpy as jnp
from jax import lax

D = 5120
FF = 1536
TOK_DEV = 1024
SLOT = 24
SOURCES = 8
EXPERTS = 8
TOKENS = 8192


def draw_slot_rows(key, part):
    keys = jax.random.split(jax.random.fold_in(key, 11), SOURCES * EXPERTS)
    picks = jax.vmap(lambda one_key: jax.random.permutation(one_key, TOK_DEV)[:SLOT])(keys)
    return picks.reshape(SOURCES, EXPERTS, SLOT).astype(jnp.int32)


def draw_expert_counts(key, part):
    hot_key, other_key = jax.random.split(jax.random.fold_in(key, 23))
    hottest = jax.random.randint(hot_key, (), 0, EXPERTS)
    others = jax.random.randint(other_key, (EXPERTS, SOURCES), max(1, SLOT // 8), SLOT // 2 + 1)
    chosen = jnp.arange(EXPERTS)[:, None] == hottest
    return jnp.where(chosen, SLOT, others).astype(jnp.int32)


def block_levels(key, shape, shards, least, largest):
    loudness, own = 1.0, jax.random.fold_in(key, 6)
    for position, shards_of in shards:
        draws = jnp.exp(jax.random.uniform(jax.random.fold_in(own, position), (shards_of,), jnp.float32, least / len(shards), largest / len(shards)))
        loudness = loudness * jnp.repeat(draws, shape[position] // shards_of).reshape([-1 if axis == position else 1 for axis in range(len(shape))])
    return loudness


def centred(key, extent, scale, most, cuts=(), kind=jnp.bfloat16):
    array = scale * jax.random.normal(key, extent, jnp.float32)
    if cuts:
        array = array * block_levels(key, extent, cuts, -0.22, 0.18)
    return jnp.clip(array, -most, most).astype(kind)


def setup_inputs(seed: int = 0) -> dict:
    key_of = jax.random.split(jax.random.key(seed), 9)
    return {
        "tokens": centred(key_of[0], (TOKENS, D), 1.0, 6.0, ((0, 8), (1, 64))),
        "out_grad": centred(key_of[1], (TOKENS, D), 1.0, 6.0, ((0, 8), (1, 64))),
        "slot_rows": draw_slot_rows(jax.random.fold_in(key_of[8], 71), 0),
        "expert_counts": draw_expert_counts(jax.random.fold_in(key_of[8], 71), 0),
        "route_prob": jnp.clip(jnp.exp(math.log(0.9) - 2.8903717 * jax.random.uniform(key_of[4], (EXPERTS, SOURCES * SLOT), jnp.float32) ** block_levels(key_of[4], (EXPERTS, SOURCES * SLOT), ((0, 8),), -0.2, 0.2)), 0.05, 0.9),
        "w_gate": centred(key_of[5], (EXPERTS, D, FF), D ** -0.5, 0.078125, ((0, 8), (1, 64))),
        "w_up": centred(key_of[6], (EXPERTS, D, FF), D ** -0.5, 0.078125, ((0, 8), (1, 64))),
        "w_down": centred(key_of[7], (EXPERTS, D, FF), FF ** -0.5, 0.15625, ((0, 8), (1, 64))),
    }


def hidden_backward(gate_sum, up_sum, down_sum, row_prob, live_mask):
    sigmoid_gate = jax.nn.sigmoid(gate_sum)
    silu_gate = gate_sum * sigmoid_gate
    hidden = lax.optimization_barrier((silu_gate * up_sum).astype(jnp.bfloat16)).astype(jnp.float32)
    row_scale = (row_prob * live_mask)[:, None]
    scaled_hidden = (hidden * row_scale).astype(jnp.bfloat16)
    hidden_grad = down_sum * row_scale
    up_act_grad = (hidden_grad * silu_gate).astype(jnp.bfloat16)
    gate_act_grad = (hidden_grad * up_sum * sigmoid_gate * (1.0 + gate_sum * (1.0 - sigmoid_gate))).astype(jnp.bfloat16)
    prob_grad = live_mask * jnp.sum(hidden * down_sum, axis=1)
    return scaled_hidden, gate_act_grad, up_act_grad, prob_grad


def reference(tokens, out_grad, slot_rows, expert_counts, route_prob, w_gate, w_up, w_down):
    offsets = (jnp.arange(SOURCES, dtype=jnp.int32) * TOK_DEV)[:, None]
    slot_index = jnp.arange(SLOT, dtype=jnp.int32)
    token_grad = jnp.zeros((TOKENS, D), jnp.float32)
    gate_grads = []
    up_grads = []
    down_grads = []
    prob_grads = []
    for expert in range(EXPERTS):
        row_index = (slot_rows[:, expert, :].astype(jnp.int32) + offsets).reshape(-1).astype(jnp.int32)
        token_rows = tokens[row_index]
        grad_rows = out_grad[row_index]
        live_mask = (slot_index[None, :] < expert_counts[expert][:, None]).reshape(-1).astype(jnp.float32)
        gate_sum = jnp.dot(token_rows, w_gate[expert], preferred_element_type=jnp.float32)
        up_sum = jnp.dot(token_rows, w_up[expert], preferred_element_type=jnp.float32)
        down_sum = jnp.dot(grad_rows, w_down[expert], preferred_element_type=jnp.float32)
        scaled_hidden, gate_act_grad, up_act_grad, prob_grad = hidden_backward(gate_sum, up_sum, down_sum, route_prob[expert], live_mask)
        gate_grads.append(jnp.dot(token_rows.T, gate_act_grad, preferred_element_type=jnp.float32))
        up_grads.append(jnp.dot(token_rows.T, up_act_grad, preferred_element_type=jnp.float32))
        down_grads.append(jnp.dot(grad_rows.T, scaled_hidden, preferred_element_type=jnp.float32))
        prob_grads.append(prob_grad)
        slot_grad = (jnp.dot(gate_act_grad, w_gate[expert].T, preferred_element_type=jnp.float32) + jnp.dot(up_act_grad, w_up[expert].T, preferred_element_type=jnp.float32)).astype(jnp.bfloat16)
        token_grad = token_grad.at[row_index].add(slot_grad.astype(jnp.float32))
    return (token_grad.astype(jnp.bfloat16), jnp.stack(gate_grads), jnp.stack(up_grads), jnp.stack(down_grads), jnp.stack(prob_grads))
```

```python
import functools

import jax
import jax.numpy as jnp
from jax import lax
from jax.experimental import pallas as pl
from jax.experimental.pallas import tpu as pltpu
from jax.sharding import PartitionSpec as P

MESH = pl.DeviceIdType.MESH
F32, BF16 = jnp.float32, jnp.bfloat16

Z = 16
EXP = 8
SLOT = 24
ROWS = EXP * SLOT
HALF = ROWS // 2
D_DEV = 80
KPAD = 128
FF = 1536
COLS = 384
NC = FF // COLS
TOK = 1024
NT = (((1,), (1,)), ((), ()))


def dot(a, b, dims=(((1,), (0,)), ((), ()))):
    return lax.dot_general(a, b, dims, preferred_element_type=F32)


def kernel(
    slots_ref, prob_ref, live_ref, tok_ref, grd_ref, wg_ref, wu_ref, wd_ref,
    tg_ref, gg_ref, ug_ref, dg_ref, pg_ref,
    onehot, sent, mine, other, weights, part, up_in, down_in, peer_out, peer_in, act, prob, prob_out, prob_in,
    back_out, back_in,
    mine_send, mine_recv, other_send, other_recv, w_send, w_recv,
    up_send, up_recv, down_send, down_recv, peer_send, peer_recv,
    ag_up_send, ag_down_send, ag_recv, pair_send, pair_recv,
    pr_up_send, pr_down_send, pr_recv, pp_send, pp_recv, back_send, back_recv,
):
    me = lax.axis_index("fsdp")
    ex = lax.axis_index("expert")
    core = lax.rem(me, 2)
    z = lax.rem(me // 2, Z)
    y = me // (2 * Z)
    d = 1 - 2 * core
    partner = me + d

    def at_z(pos):
        return (y * Z + pos) * 2 + core

    def wrap(pos):
        return lax.rem(pos + 2 * Z, Z)

    ahead, behind = at_z(wrap(z + d)), at_z(wrap(z - d))
    y_peer = ((1 - y) * Z + z) * 2 + core

    def remote(src, dst, send, recv, f, e):
        return pltpu.make_async_remote_copy(
            src_ref=src, dst_ref=dst, send_sem=send, recv_sem=recv,
            device_id={"fsdp": f, "expert": e}, device_id_type=MESH)

    barrier = pltpu.get_barrier_semaphore()
    for f in (partner, ahead, behind, y_peer):
        pl.semaphore_signal(barrier, inc=1, device_id={"fsdp": f, "expert": ex}, device_id_type=MESH)
    for k in range(1, EXP):
        e = lax.rem(ex + k, EXP)
        for f in (me, partner):
            pl.semaphore_signal(barrier, inc=1, device_id={"fsdp": f, "expert": e}, device_id_type=MESH)

    columns = lax.broadcasted_iota(jnp.int32, (ROWS, TOK), 1)
    onehot[...] = jnp.where(slots_ref[...] == columns, 1.0, 0.0).astype(BF16)
    for i, src in enumerate((tok_ref, grd_ref)):
        rows = dot(onehot[...], src[...], NT)
        rows = jnp.concatenate([rows, jnp.zeros((ROWS, KPAD - D_DEV), F32)], axis=1)
        sent[:, i] = rows.reshape(EXP, SLOT, KPAD).astype(BF16)
    pad = jnp.zeros((KPAD - D_DEV, FF), BF16)
    for i, w in enumerate((wg_ref, wu_ref, wd_ref)):
        weights[i, 0:D_DEV] = w[...]
        weights[i, D_DEV:KPAD] = pad
        weights[i, KPAD + D_DEV:2 * KPAD] = pad

    pl.semaphore_wait(barrier, 4 + 2 * (EXP - 1))

    def mine_copy(k):
        e = lax.rem(ex + k, EXP)
        return remote(sent.at[e], mine.at[ex], mine_send.at[e], mine_recv.at[ex], me, e)

    def other_copy(k):
        e = lax.rem(ex + k, EXP)
        return remote(sent.at[e], other.at[ex], other_send.at[e], other_recv.at[ex], partner, e)

    def mine_in(k):
        e = lax.rem(ex + k, EXP)
        return remote(sent.at[e], mine.at[e], mine_send.at[e], mine_recv.at[e], me, e)

    def other_in(k):
        e = lax.rem(ex + k, EXP)
        return remote(sent.at[e], other.at[e], other_send.at[e], other_recv.at[e], partner, e)

    def w_copy(i):
        src = (wg_ref, wu_ref, wd_ref)[i]
        return remote(src, weights.at[i, pl.ds(KPAD, D_DEV)], w_send.at[i], w_recv.at[i], partner, ex)

    for k in range(EXP):
        other_copy(k).start()
    for k in range(1, EXP):
        mine_copy(k).start()
    for i in range(3):
        w_copy(i).start()
    mine[ex] = sent[ex]
    for i in range(3):
        w_copy(i).wait_recv()
    for k in range(EXP):
        other_in(k).wait_recv()
    for k in range(1, EXP):
        mine_in(k).wait_recv()

    own_rows = [
        jnp.concatenate([
            mine[pl.ds(4 * core, 4), i].astype(F32).reshape(HALF, KPAD),
            other[pl.ds(4 * core, 4), i].astype(F32).reshape(HALF, KPAD),
        ], axis=1).astype(BF16)
        for i in range(2)
    ]
    for c in range(NC):
        for i in range(3):
            out = dot(own_rows[i // 2], weights[i, :, c * COLS:(c + 1) * COLS])
            for r in range(4):
                part[r * NC + c, i] = out[r * SLOT:(r + 1) * SLOT]

    def up_copy(s, i, src):
        return remote(src, up_in.at[s, i], up_send.at[s, i], up_recv.at[s, i], ahead, ex)

    def down_copy(s, i, src):
        return remote(src, down_in.at[s, i], down_send.at[s, i], down_recv.at[s, i], behind, ex)

    for i in range(3):
        up_copy(0, i, part.at[wrap(z + 8 * d), i]).start()
        down_copy(0, i, part.at[wrap(z - 7 * d), i]).start()

    def up_step(s, i):
        up_copy(s - 1, i, up_in.at[s - 1, i]).wait_recv()
        up_in[s - 1, i] = up_in[s - 1, i] + part[wrap(z + d * (8 - s)), i]
        up_copy(s, i, up_in.at[s - 1, i]).start()

    def down_step(s, i):
        down_copy(s - 1, i, down_in.at[s - 1, i]).wait_recv()
        down_in[s - 1, i] = down_in[s - 1, i] + part[wrap(z - d * (7 - s)), i]
        down_copy(s, i, down_in.at[s - 1, i]).start()

    def ring_step(s, _):
        for i in range(3):
            up_step(s, i)
            down_step(s, i)
        return 0

    lax.fori_loop(1, 7, ring_step, 0)
    for i in range(3):
        up_step(7, i)

    def peer_copy(i):
        return remote(peer_out.at[i], peer_in.at[i], peer_send.at[i], peer_recv.at[i], y_peer, ex)

    for i in range(3):
        down_copy(6, i, down_in.at[6, i]).wait_recv()
        up_copy(7, i, up_in.at[7, i]).wait_recv()
        peer_out[i] = (up_in[7, i] + down_in[6, i]) + part[z, i]
        peer_copy(i).start()
    for i in range(3):
        peer_copy(i).wait_recv()
    gate, up, down = (peer_out[i] + peer_in[i] for i in range(3))

    source = 4 * core + z // NC
    live = live_ref[source]
    scale = prob_ref[source] * live
    sigmoid = jax.nn.sigmoid(gate)
    silu = gate * sigmoid
    hidden = (silu * up).astype(BF16).astype(F32)
    hidden_grad = down * scale
    act[core, z, 0] = (hidden_grad * up * sigmoid * (1.0 + gate * (1.0 - sigmoid))).astype(BF16)
    act[core, z, 1] = (hidden_grad * silu).astype(BF16)
    act[core, z, 2] = (hidden * scale).astype(BF16)
    prob[z] = jnp.broadcast_to(live * jnp.sum(hidden * down, axis=1, keepdims=True), (SLOT, 128))

    def ag_up(s, i):
        owner = wrap(z - d * s)
        return remote(act.at[core, owner, i], act.at[core, owner, i], ag_up_send.at[s, i], ag_recv.at[owner, i], ahead, ex)

    def ag_down(s, i):
        owner = wrap(z + d * s)
        return remote(act.at[core, owner, i], act.at[core, owner, i], ag_down_send.at[s, i], ag_recv.at[owner, i], behind, ex)

    def pair_copy(half, owner, i):
        return remote(act.at[half, owner, i], act.at[half, owner, i], pair_send.at[owner, i], pair_recv.at[owner, i], partner, ex)

    def pr_up(s):
        owner = wrap(z - d * s)
        return remote(prob.at[owner], prob.at[owner], pr_up_send.at[s], pr_recv.at[owner], ahead, ex)

    def pr_down(s):
        owner = wrap(z + d * s)
        return remote(prob.at[owner], prob.at[owner], pr_down_send.at[s], pr_recv.at[owner], behind, ex)

    for i in range(3):
        ag_up(0, i).start()
        ag_down(0, i).start()
    pr_up(0).start()
    pr_down(0).start()
    for i in range(3):
        pair_copy(core, z, i).start()

    def gather_step(s, _):
        for i in range(3):
            ag_up(s, i).wait_recv()
            ag_up(s, i).start()
            ag_down(s, i).wait_recv()

            @pl.when(s < 7)
            def _():
                ag_down(s, i).start()

        for i in range(3):
            pair_copy(core, wrap(z - d * s), i).start()
            pair_copy(core, wrap(z + d * s), i).start()

        @pl.when(s < 4)
        def _():
            pr_up(s).wait_recv()
            pr_down(s).wait_recv()

            @pl.when(s < 3)
            def _():
                pr_up(s).start()
                pr_down(s).start()

        return 0

    lax.fori_loop(1, 8, gather_step, 0)
    for i in range(3):
        ag_up(8, i).wait_recv()
        pair_copy(core, wrap(z + 8), i).start()

    group = z // NC
    prob_out[...] = sum(prob[group * NC + c] for c in range(NC))
    pp = remote(prob_out, prob_in, pp_send, pp_recv, partner, ex)
    pp.start()

    def pair_wait(owner, _):
        for i in range(3):
            pair_copy(1 - core, owner, i).wait_recv()
        return 0

    lax.fori_loop(0, Z, pair_wait, 0)

    def full(i, c):
        return jnp.concatenate(
            [act[h, r * NC + c, i].astype(F32) for h in range(2) for r in range(4)], axis=0).astype(BF16)

    acts = [[full(i, c) for c in range(NC)] for i in range(3)]
    slot_grad = jnp.zeros((ROWS, D_DEV), F32)
    for c in range(NC):
        cols = slice(c * COLS, (c + 1) * COLS)
        slot_grad += dot(acts[0][c], wg_ref[:, cols], NT)
        slot_grad += dot(acts[1][c], wu_ref[:, cols], NT)
    slot_grad = jnp.concatenate([slot_grad, jnp.zeros((ROWS, KPAD - D_DEV), F32)], axis=1)
    back_out[...] = slot_grad.reshape(EXP, SLOT, KPAD).astype(BF16)

    def back_copy(k):
        e = lax.rem(ex + k, EXP)
        return remote(back_out.at[e], back_in.at[ex], back_send.at[e], back_recv.at[ex], me, e)

    def back_wait(k):
        e = lax.rem(ex + k, EXP)
        return remote(back_out.at[e], back_in.at[e], back_send.at[e], back_recv.at[e], me, e)

    for k in range(1, EXP):
        back_copy(k).start()
    back_in[ex] = back_out[ex]

    rows_t = [mine[:, i].astype(F32).reshape(ROWS, KPAD).T.astype(BF16) for i in range(2)]
    for i, out in enumerate((gg_ref, ug_ref, dg_ref)):
        for c in range(NC):
            out[:, c * COLS:(c + 1) * COLS] = dot(rows_t[i // 2], acts[i][c])[:D_DEV]

    pp.wait()
    total = jnp.where(core == y, prob_out[...], prob_in[...])
    first = 3 * (lax.rem(z, NC) * 2 + core)
    row = lax.broadcasted_iota(jnp.int32, (SLOT, 128), 0)
    lane = lax.broadcasted_iota(jnp.int32, (SLOT, 128), 1)
    picked = jnp.sum(jnp.where(row == first + lane, total, 0.0), axis=0, keepdims=True)
    pg_ref[...] = picked[:, :3]

    for k in range(1, EXP):
        back_wait(k).wait_recv()
    back_t = back_in[...].astype(F32).reshape(ROWS, KPAD).T.astype(BF16)
    tg_ref[...] = dot(back_t, onehot[...])[:D_DEV].astype(BF16)

    for k in range(EXP):
        other_copy(k).wait_send()
    for k in range(1, EXP):
        mine_copy(k).wait_send()
        back_copy(k).wait_send()
    for i in range(3):
        w_copy(i).wait_send()
        peer_copy(i).wait_send()
    for s in range(3):
        pr_up(s).wait_send()
        pr_down(s).wait_send()

    def drain(s, _):
        for i in range(3):
            up_copy(s, i, up_in.at[s, i]).wait_send()
            ag_up(s, i).wait_send()

            @pl.when(s < 7)
            def _():
                down_copy(s, i, down_in.at[s, i]).wait_send()
                ag_down(s, i).wait_send()

        return 0

    lax.fori_loop(0, 8, drain, 0)

    def pair_drain(owner, _):
        for i in range(3):
            pair_copy(core, owner, i).wait_send()
        return 0

    lax.fori_loop(0, Z, pair_drain, 0)


def local(tokens, out_grad, slot_rows, expert_counts, route_prob, w_gate, w_up, w_down):
    slots = slot_rows[0].reshape(ROWS, 1)
    live = (jnp.arange(SLOT, dtype=jnp.int32)[None, :] < expert_counts[0][:, None]).astype(F32)[:, :, None]
    prob = route_prob[0].reshape(EXP, SLOT, 1)
    vmem = pl.BlockSpec(memory_space=pltpu.VMEM)
    dma = pltpu.SemaphoreType.DMA
    grad = jax.ShapeDtypeStruct((D_DEV, FF), F32)
    tg, gg, ug, dg, pg = pl.pallas_call(
        kernel,
        out_shape=(jax.ShapeDtypeStruct((D_DEV, TOK), BF16), grad, grad, grad, jax.ShapeDtypeStruct((1, 3), F32)),
        in_specs=[vmem] * 8,
        out_specs=(vmem,) * 5,
        scratch_shapes=[
            pltpu.VMEM((ROWS, TOK), BF16),
            pltpu.VMEM((EXP, 2, SLOT, KPAD), BF16),
            pltpu.VMEM((EXP, 2, SLOT, KPAD), BF16),
            pltpu.VMEM((EXP, 2, SLOT, KPAD), BF16),
            pltpu.VMEM((3, 2 * KPAD, FF), BF16),
            pltpu.VMEM((Z, 3, SLOT, COLS), F32),
            pltpu.VMEM((8, 3, SLOT, COLS), F32),
            pltpu.VMEM((7, 3, SLOT, COLS), F32),
            pltpu.VMEM((3, SLOT, COLS), F32),
            pltpu.VMEM((3, SLOT, COLS), F32),
            pltpu.VMEM((2, Z, 3, SLOT, COLS), BF16),
            pltpu.VMEM((Z, SLOT, 128), F32),
            pltpu.VMEM((SLOT, 128), F32),
            pltpu.VMEM((SLOT, 128), F32),
            pltpu.VMEM((EXP, SLOT, KPAD), BF16),
            pltpu.VMEM((EXP, SLOT, KPAD), BF16),
            dma((EXP,)), dma((EXP,)), dma((EXP,)), dma((EXP,)), dma((3,)), dma((3,)),
            dma((8, 3)), dma((8, 3)), dma((7, 3)), dma((7, 3)), dma((3,)), dma((3,)),
            dma((8, 3)), dma((7, 3)), dma((Z, 3)), dma((Z, 3)), dma((Z, 3)),
            dma((3,)), dma((3,)), dma((Z,)), dma, dma, dma((EXP,)), dma((EXP,)),
        ],
        compiler_params=pltpu.CompilerParams(collective_id=0, has_side_effects=True),
    )(slots, prob, live, tokens.T, out_grad.T, w_gate[0], w_up[0], w_down[0])
    return tg.T, gg[None], ug[None], dg[None], pg


def solution(mesh):
    return jax.shard_map(
        local,
        mesh=mesh,
        in_specs=(
            P("expert", "fsdp"),
            P("expert", "fsdp"),
            P("expert", None, None),
            P("expert", None),
            P("expert", None),
            P("expert", "fsdp", None),
            P("expert", "fsdp", None),
            P("expert", "fsdp", None),
        ),
        out_specs=(
            P("expert", "fsdp"),
            P("expert", "fsdp", None),
            P("expert", "fsdp", None),
            P("expert", "fsdp", None),
            P("expert", "fsdp"),
        ),
        check_vma=False,
    )
```

```python
import jax
import jax.numpy as jnp
from jax import lax
from jax.experimental import pallas as pl
from jax.experimental.pallas import tpu as pltpu
from jax.sharding import PartitionSpec as P

MESH = pl.DeviceIdType.MESH
F32, BF16 = jnp.float32, jnp.bfloat16

Z = 16
EXP = 8
SLOT = 24
ROWS = EXP * SLOT
HALF = ROWS // 2
D_DEV = 80
KPAD = 128
FF = 1536
COLS = 384
NC = FF // COLS
TOK = 1024
SUB = 1
NB = 4
NT = (((1,), (1,)), ((), ()))


def dot(a, b, dims=(((1,), (0,)), ((), ()))):
    return lax.dot_general(a, b, dims, preferred_element_type=F32)


def slot_column(slots_ref):
    wide = jnp.concatenate([slots_ref[0].astype(F32), jnp.zeros((EXP, KPAD - SLOT), F32)], axis=1)
    tall = wide.T
    return jnp.concatenate([tall[:SLOT, e:e + 1] for e in range(EXP)], axis=0)


def one_hot(slots_ref, first, width):
    columns = lax.broadcasted_iota(jnp.int32, (ROWS, width), 1) + first
    return jnp.where(slot_column(slots_ref) == columns.astype(F32), 1.0, 0.0).astype(BF16)


def pad_features(rows):
    return jnp.concatenate([rows, jnp.zeros((ROWS, KPAD - D_DEV), F32)], axis=1)


def kernel(
    slots_ref, prob_ref, counts_ref, tok_ref, grd_ref, wg_ref, wu_ref, wd_ref,
    acts_ref, rows_ref, back_ref, pg_ref,
    sent, mine, other, weights, part, up_in, down_in, fin_in, own_in, act, acts, rows_t,
    prob, prob_out, prob_in, back_out, back_in,
    mine_send, mine_recv, other_send, other_recv, w_send, w_recv,
    up_send, up_recv, down_send, down_recv, fin_send, fin_recv, own_send, own_recv,
    ag_send, ag_recv, pair_send, pair_recv, pr_send, pr_recv, pp_send, pp_recv, back_send, back_recv, out_sem,
):
    me = lax.axis_index("fsdp")
    ex = lax.axis_index("expert")
    core = lax.rem(me, 2)
    z = lax.rem(me // 2, Z)
    y = me // (2 * Z)
    d = 1 - 2 * core
    partner = me + d

    def at_z(pos, plane=None):
        return ((y if plane is None else plane) * Z + pos) * 2 + core

    def wrap(pos):
        return lax.rem(pos + 2 * Z, Z)

    near = [at_z(wrap(z + d)), at_z(wrap(z - d))]
    far = [at_z(wrap(z + 2 * d)), at_z(wrap(z - 2 * d))]
    cross = [at_z(wrap(z + d), 1 - y), at_z(wrap(z - d), 1 - y)]
    y_peer = at_z(z, 1 - y)
    sign = (d, -d)
    pending = []

    def remote(src, dst, send, recv, f, e=None):
        return pltpu.make_async_remote_copy(
            src_ref=src, dst_ref=dst, send_sem=send, recv_sem=recv,
            device_id={"fsdp": f, "expert": ex if e is None else e}, device_id_type=MESH)

    def go(copy):
        copy.start()
        pending.append(copy)

    barrier = pltpu.get_barrier_semaphore()
    friends = [partner, y_peer] + near + far + cross
    for k in range(1, EXP):
        e = lax.rem(ex + k, EXP)
        for f in (me, partner):
            pl.semaphore_signal(barrier, inc=1, device_id={"fsdp": f, "expert": e}, device_id_type=MESH)
    for f in friends:
        pl.semaphore_signal(barrier, inc=1, device_id={"fsdp": f, "expert": ex}, device_id_type=MESH)

    table = one_hot(slots_ref, 0, TOK)
    for i, src in enumerate((tok_ref, grd_ref)):
        sent[:, i] = pad_features(dot(table, src[...], NT)).reshape(EXP, SLOT, KPAD).astype(BF16)
    pad = jnp.zeros((KPAD - D_DEV, FF), BF16)
    for i, w in enumerate((wg_ref, wu_ref, wd_ref)):
        weights[i, 0:D_DEV] = w[...]
        weights[i, D_DEV:KPAD] = pad
        weights[i, KPAD + D_DEV:2 * KPAD] = pad

    pl.semaphore_wait(barrier, len(friends) + 2 * (EXP - 1))

    def peer_expert(k):
        return lax.rem(ex + k, EXP)

    for k in range(EXP):
        e = peer_expert(k)
        go(remote(sent.at[e], other.at[ex], other_send.at[e], other_recv.at[ex], partner, e))
        if k:
            go(remote(sent.at[e], mine.at[ex], mine_send.at[e], mine_recv.at[ex], me, e))
    w_copies = [
        remote(w, weights.at[i, pl.ds(KPAD, D_DEV)], w_send.at[i], w_recv.at[i], partner)
        for i, w in enumerate((wg_ref, wu_ref, wd_ref))]
    for copy in w_copies:
        go(copy)
    mine[ex] = sent[ex]
    for copy in w_copies:
        copy.wait_recv()
    for k in range(EXP):
        e = peer_expert(k)
        remote(sent.at[e], other.at[e], other_send.at[e], other_recv.at[e], partner, e).wait_recv()
        if k:
            remote(sent.at[e], mine.at[e], mine_send.at[e], mine_recv.at[e], me, e).wait_recv()

    own_rows = [
        jnp.concatenate([
            mine[pl.ds(4 * core, 4), i].astype(F32).reshape(HALF, KPAD),
            other[pl.ds(4 * core, 4), i].astype(F32).reshape(HALF, KPAD),
        ], axis=1).astype(BF16)
        for i in range(2)
    ]
    for c in range(NC):
        for i in range(3):
            out = dot(own_rows[i // 2], weights[i, :, c * COLS:(c + 1) * COLS])
            for r in range(4):
                for g in range(3):
                    part[r * NC + c, g * 3 + i] = out[r * SLOT + g * 8:r * SLOT + g * 8 + 8]

    subs = [(q, pl.ds(q, SUB)) for q in range(0, 9, SUB)]

    def up_copy(a, q, block, src, skip=False):
        return remote(src, up_in.at[a - 1, block], up_send.at[a - 1, q], up_recv.at[a - 1, q], far[0] if skip else near[0])

    def down_copy(a, q, block, src):
        return remote(src, down_in.at[a - 1, block], down_send.at[a - 1, q], down_recv.at[a - 1, q], near[1])

    def fin_copy(way, other_plane, q, block, src):
        f = (cross if other_plane else near)[way]
        return remote(src, fin_in.at[way, other_plane, block], fin_send.at[way, other_plane, q],
                      fin_recv.at[way, other_plane, q], f)

    def own_copy(q, block):
        return remote(part.at[z, block], own_in.at[block], own_send.at[q], own_recv.at[q], y_peer)

    for q, block in subs:
        up_copy(8, q, block, part.at[wrap(z + 8 * d), block], True).start()
        up_copy(7, q, block, part.at[wrap(z + 7 * d), block]).start()
        down_copy(7, q, block, part.at[wrap(z - 7 * d), block]).start()
    for q, block in subs:
        own_copy(q, block).start()

    for i in range(2):
        rows_t[i] = mine[:, i].astype(F32).reshape(ROWS, KPAD).T.astype(BF16)
    rows_out = pltpu.make_async_copy(rows_t, rows_ref, out_sem.at[0])
    rows_out.start()

    def up_add(j, q, block):
        up_copy(j + 1, q, block, up_in.at[j, block]).wait_recv()
        up_in[j, block] = up_in[j, block] + part[wrap(z + d * j), block]

    def down_add(j, q, block):
        down_copy(j + 1, q, block, down_in.at[j, block]).wait_recv()
        down_in[j, block] = down_in[j, block] + part[wrap(z - d * j), block]

    for q, block in subs:
        down_add(6, q, block)
        down_copy(6, q, block, down_in.at[6, block]).start()
        up_copy(8, q, block, up_in.at[7, block], True).wait_recv()
        up_add(6, q, block)
        up_in[6, block] = up_in[6, block] + up_in[7, block]
        up_copy(6, q, block, up_in.at[6, block]).start()

    def ring_step(t, _):
        j = 5 - t
        for q, block in subs:
            down_add(j, q, block)
            down_copy(j, q, block, down_in.at[j, block]).start()
            up_add(j, q, block)
            up_copy(j, q, block, up_in.at[j, block]).start()
        return 0

    lax.fori_loop(0, 4, ring_step, 0)
    for q, block in subs:
        down_add(1, q, block)
        for other_plane in (1, 0):
            fin_copy(1, other_plane, q, block, down_in.at[1, block]).start()
        up_add(1, q, block)
        for other_plane in (1, 0):
            fin_copy(0, other_plane, q, block, up_in.at[1, block]).start()

    source = 4 * core + z // NC
    k8 = lax.broadcasted_iota(jnp.int32, (8, 1), 0)
    lane = lax.broadcasted_iota(jnp.int32, (8, ROWS), 1)
    count = jnp.sum(jnp.where(lax.broadcasted_iota(jnp.int32, (1, EXP), 1) == source, counts_ref[...].astype(F32), 0.0),
                    axis=1, keepdims=True)
    spot = lax.broadcasted_iota(jnp.int32, (8, 128), 1)

    def ag_copy(way, a, g, two):
        owner = wrap(z - sign[way] * a)
        return remote(act.at[core, owner, g], act.at[core, owner, g], ag_send.at[way, a + (2 if two else 1) - 1, g],
                      ag_recv.at[owner, g], (far if two else near)[way])

    def ag_arrival(way, a, g):
        owner = wrap(z - sign[way] * a)
        return remote(act.at[core, owner, g], act.at[core, owner, g], ag_send.at[way, 0, g], ag_recv.at[owner, g], near[way])

    def pair_copy(half, owner, g):
        return remote(act.at[half, owner, g], act.at[half, owner, g], pair_send.at[owner, g], pair_recv.at[owner, g], partner)

    def pr_copy(way, a, two):
        owner = wrap(z - sign[way] * a)
        return remote(prob.at[owner], prob.at[owner], pr_send.at[way, a + (2 if two else 1) - 1], pr_recv.at[owner],
                      (far if two else near)[way])

    last = (8, 7)

    def hand_on(a, g):
        for two in (True, False):
            for way in range(2):
                if a + (2 if two else 1) <= last[way]:
                    go(ag_copy(way, a, g, two))

    tile = jnp.zeros((8, 128), F32)
    for g in range(3):
        sums = []
        for i in range(3):
            q = (g * 3 + i) // SUB * SUB
            block = pl.ds(q, SUB)
            if (g * 3 + i) % SUB == 0:
                own_copy(q, block).wait_recv()
                for way in range(2):
                    for other_plane in range(2):
                        fin_copy(way, other_plane, q, block, fin_in.at[way, other_plane, block]).wait_recv()
            n = g * 3 + i
            here = (fin_in[0, 0, n] + fin_in[1, 0, n]) + part[z, n]
            there = (fin_in[0, 1, n] + fin_in[1, 1, n]) + own_in[n]
            sums.append(here + there)
        gate, up, down = sums
        slot = k8 + 8 * g
        live = (slot.astype(F32) < count).astype(F32)
        scale = live * jnp.sum(jnp.where(lane == slot + SLOT * source, prob_ref[...], 0.0), axis=1, keepdims=True)
        sigmoid = jax.nn.sigmoid(gate)
        silu = gate * sigmoid
        hidden = (silu * up).astype(BF16).astype(F32)
        hidden_grad = down * scale
        act[core, z, g, 0] = (hidden_grad * up * sigmoid * (1.0 + gate * (1.0 - sigmoid))).astype(BF16)
        act[core, z, g, 1] = (hidden_grad * silu).astype(BF16)
        act[core, z, g, 2] = (hidden * scale).astype(BF16)
        hand_on(0, g)
        go(pair_copy(core, z, g))
        tile += jnp.where(spot == g, live * jnp.sum(hidden * down, axis=1, keepdims=True), 0.0)
    prob[z] = tile
    for way in range(2):
        for two in (True, False):
            go(pr_copy(way, 0, two))

    for t in range(1, 5):
        for g in range(3):
            for way in range(2):
                if 2 * t <= last[way]:
                    ag_arrival(way, 2 * t, g).wait_recv()
            hand_on(2 * t, g)
            for way in range(2):
                if 2 * t <= last[way]:
                    go(pair_copy(core, wrap(z - sign[way] * 2 * t), g))
        for g in range(3):
            for way in range(2):
                ag_arrival(way, 2 * t - 1, g).wait_recv()
                go(pair_copy(core, wrap(z - sign[way] * (2 * t - 1)), g))
        if t == 1:
            for way in range(2):
                pr_copy(way, 2, False).wait_recv()
                go(pr_copy(way, 2, False))
                pr_copy(way, 1, False).wait_recv()
        if t == 2:
            for way in range(2):
                pr_copy(way, 3, False).wait_recv()
            group = z // NC
            prob_out[...] = sum(prob[group * NC + c] for c in range(NC))
            pp = remote(prob_out, prob_in, pp_send, pp_recv, partner)
            go(pp)

    def pair_wait(owner, _):
        for g in range(3):
            pair_copy(1 - core, owner, g).wait_recv()
        return 0

    lax.fori_loop(0, Z, pair_wait, 0)

    slot_grad = jnp.zeros((ROWS, D_DEV), F32)
    for c in range(NC):
        cols = slice(c * COLS, (c + 1) * COLS)
        for i in range(3):
            full = jnp.concatenate(
                [act[h, r * NC + c, g, i].astype(F32) for h in range(2) for r in range(4) for g in range(3)],
                axis=0).astype(BF16)
            acts[i, :, cols] = full
            if i < 2:
                slot_grad += dot(full, (wg_ref, wu_ref)[i][:, cols], NT)
    back_out[...] = pad_features(slot_grad).reshape(EXP, SLOT, KPAD).astype(BF16)
    for k in range(1, EXP):
        e = peer_expert(k)
        go(remote(back_out.at[e], back_in.at[ex], back_send.at[e], back_recv.at[ex], me, e))
    acts_out = pltpu.make_async_copy(acts, acts_ref, out_sem.at[1])
    acts_out.start()
    back_in[ex] = back_out[ex]

    pp.wait_recv()
    total = jnp.where(core == y, prob_out[...], prob_in[...])
    place = lax.broadcasted_iota(jnp.int32, (8, 128), 0) + 8 * spot
    first = 3 * (lax.rem(z, NC) * 2 + core)
    picked = [jnp.sum(jnp.where(place == first + j, total, 0.0), axis=(0, 1), keepdims=True) for j in range(3)]
    pg_ref[...] = jnp.concatenate(picked, axis=1)

    for copy in pending:
        copy.wait_send()

    def drain(a, _):
        for q, block in subs:
            up_copy(a, q, block, up_in.at[a - 1, block]).wait_send()
            down_copy(a, q, block, down_in.at[a - 1, block]).wait_send()
        return 0

    lax.fori_loop(2, 8, drain, 0)
    for q, block in subs:
        up_copy(8, q, block, up_in.at[7, block], True).wait_send()
        own_copy(q, block).wait_send()
        for way in range(2):
            for other_plane in range(2):
                fin_copy(way, other_plane, q, block, fin_in.at[way, other_plane, block]).wait_send()
    for k in range(1, EXP):
        e = peer_expert(k)
        remote(back_out.at[e], back_in.at[e], back_send.at[e], back_recv.at[e], me, e).wait_recv()
    back_out_copy = pltpu.make_async_copy(back_in, back_ref, out_sem.at[2])
    back_out_copy.start()
    rows_out.wait()
    acts_out.wait()
    back_out_copy.wait()


def last_kernel(slots_ref, acts_ref, rows_ref, back_ref, tg_ref, gg_ref, ug_ref, dg_ref):
    for i, out in enumerate((gg_ref, ug_ref, dg_ref)):
        out[0] = dot(rows_ref[i // 2], acts_ref[i])[:D_DEV]
    back_t = back_ref[...].astype(F32).reshape(ROWS, KPAD).T.astype(BF16)
    width = TOK // NB
    table = one_hot(slots_ref, pl.program_id(0) * width, width)
    tg_ref[...] = dot(back_t, table)[:D_DEV].astype(BF16)


def local(tokens, out_grad, slot_rows, expert_counts, route_prob, w_gate, w_up, w_down):
    vmem = pl.BlockSpec(memory_space=pltpu.VMEM)
    hbm = pl.BlockSpec(memory_space=pl.ANY)
    dma = pltpu.SemaphoreType.DMA
    shape = jax.ShapeDtypeStruct
    acts, rows, back, pg = pl.pallas_call(
        kernel,
        out_shape=(shape((3, ROWS, FF), BF16), shape((2, KPAD, ROWS), BF16), shape((EXP, SLOT, KPAD), BF16), shape((1, 3), F32)),
        in_specs=[vmem] * 8,
        out_specs=(hbm, hbm, hbm, vmem),
        scratch_shapes=[
            pltpu.VMEM((EXP, 2, SLOT, KPAD), BF16),
            pltpu.VMEM((EXP, 2, SLOT, KPAD), BF16),
            pltpu.VMEM((EXP, 2, SLOT, KPAD), BF16),
            pltpu.VMEM((3, 2 * KPAD, FF), BF16),
            pltpu.VMEM((Z, 9, 8, COLS), F32),
            pltpu.VMEM((8, 9, 8, COLS), F32),
            pltpu.VMEM((7, 9, 8, COLS), F32),
            pltpu.VMEM((2, 2, 9, 8, COLS), F32),
            pltpu.VMEM((9, 8, COLS), F32),
            pltpu.VMEM((2, Z, 3, 3, 8, COLS), BF16),
            pltpu.VMEM((3, ROWS, FF), BF16),
            pltpu.VMEM((2, KPAD, ROWS), BF16),
            pltpu.VMEM((Z, 8, 128), F32),
            pltpu.VMEM((8, 128), F32),
            pltpu.VMEM((8, 128), F32),
            pltpu.VMEM((EXP, SLOT, KPAD), BF16),
            pltpu.VMEM((EXP, SLOT, KPAD), BF16),
            dma((EXP,)), dma((EXP,)), dma((EXP,)), dma((EXP,)), dma((3,)), dma((3,)),
            dma((8, 9)), dma((8, 9)), dma((7, 9)), dma((7, 9)), dma((2, 2, 9)), dma((2, 2, 9)), dma((9,)), dma((9,)),
            dma((2, 8, 3)), dma((Z, 3)), dma((Z, 3)), dma((Z, 3)), dma((2, 3)), dma((Z,)), dma, dma,
            dma((EXP,)), dma((EXP,)), dma((3,)),
        ],
        compiler_params=pltpu.CompilerParams(collective_id=0, has_side_effects=True),
    )(slot_rows, route_prob, expert_counts, tokens.T, out_grad.T, w_gate[0], w_up[0], w_down[0])
    grad = shape((1, D_DEV, FF), F32)
    grad_spec = pl.BlockSpec((1, D_DEV, FF // NB), lambda n: (0, 0, n))
    tg, gg, ug, dg = pl.pallas_call(
        last_kernel,
        grid=(NB,),
        out_shape=(shape((D_DEV, TOK), BF16), grad, grad, grad),
        in_specs=[
            pl.BlockSpec((1, EXP, SLOT), lambda n: (0, 0, 0)),
            pl.BlockSpec((3, ROWS, FF // NB), lambda n: (0, 0, n)),
            pl.BlockSpec((2, KPAD, ROWS), lambda n: (0, 0, 0)),
            pl.BlockSpec((EXP, SLOT, KPAD), lambda n: (0, 0, 0)),
        ],
        out_specs=(pl.BlockSpec((D_DEV, TOK // NB), lambda n: (0, n)), grad_spec, grad_spec, grad_spec),
    )(slot_rows, acts, rows, back)
    return tg.T, gg, ug, dg, pg


def solution(mesh):
    return jax.shard_map(
        local,
        mesh=mesh,
        in_specs=(
            P("expert", "fsdp"),
            P("expert", "fsdp"),
            P("expert", None, None),
            P("expert", None),
            P("expert", None),
            P("expert", "fsdp", None),
            P("expert", "fsdp", None),
            P("expert", "fsdp", None),
        ),
        out_specs=(
            P("expert", "fsdp"),
            P("expert", "fsdp", None),
            P("expert", "fsdp", None),
            P("expert", "fsdp", None),
            P("expert", "fsdp"),
        ),
        check_vma=False,
    )
```

```python
import jax
import jax.numpy as jnp
from jax import lax
from jax.experimental import pallas as pl
from jax.experimental.pallas import tpu as pltpu
from jax.sharding import PartitionSpec as P

MESH = pl.DeviceIdType.MESH
F32, BF16 = jnp.float32, jnp.bfloat16

Z = 16
EXP = 8
SLOT = 24
ROWS = EXP * SLOT
HALF = ROWS // 2
D_DEV = 80
KPAD = 128
FF = 1536
COLS = 384
NC = FF // COLS
TOK = 1024
SUB = 1
NT = (((1,), (1,)), ((), ()))


def dot(a, b, dims=(((1,), (0,)), ((), ()))):
    return lax.dot_general(a, b, dims, preferred_element_type=F32)


def slot_column(slots_ref):
    wide = jnp.concatenate([slots_ref[0].astype(F32), jnp.zeros((EXP, KPAD - SLOT), F32)], axis=1)
    tall = wide.T
    return jnp.concatenate([tall[:SLOT, e:e + 1] for e in range(EXP)], axis=0)


def one_hot(slots_ref):
    columns = lax.broadcasted_iota(jnp.int32, (ROWS, TOK), 1)
    return jnp.where(slot_column(slots_ref) == columns.astype(F32), 1.0, 0.0).astype(BF16)


def pad_features(rows):
    return jnp.concatenate([rows, jnp.zeros((ROWS, KPAD - D_DEV), F32)], axis=1)


def kernel(
    slots_ref, prob_ref, counts_ref, tok_ref, grd_ref, wg_ref, wu_ref, wd_ref,
    acts_ref, rows_ref, back_ref, pg_ref,
    feats, sent, mine, other, weights, part, up_in, down_in, fin_in, own_in, act, acts, rows_t,
    prob, prob_out, prob_in, back_out, back_in,
    mine_send, mine_recv, other_send, other_recv, w_send, w_recv,
    up_send, up_recv, down_send, down_recv, fin_send, fin_recv, own_send, own_recv,
    ag_send, ag_recv, pair_send, pair_recv, pr_send, pr_recv, pp_send, pp_recv, back_send, back_recv, in_sem, out_sem,
):
    me = lax.axis_index("fsdp")
    ex = lax.axis_index("expert")
    core = lax.rem(me, 2)
    z = lax.rem(me // 2, Z)
    y = me // (2 * Z)
    d = 1 - 2 * core
    partner = me + d

    def at_z(pos, plane=None):
        return ((y if plane is None else plane) * Z + pos) * 2 + core

    def wrap(pos):
        return lax.rem(pos + 2 * Z, Z)

    near = [at_z(wrap(z + d)), at_z(wrap(z - d))]
    far = [at_z(wrap(z + 2 * d)), at_z(wrap(z - 2 * d))]
    cross = [at_z(wrap(z + d), 1 - y), at_z(wrap(z - d), 1 - y)]
    y_peer = at_z(z, 1 - y)
    sign = (d, -d)
    pending = []

    def remote(src, dst, send, recv, f, e=None):
        return pltpu.make_async_remote_copy(
            src_ref=src, dst_ref=dst, send_sem=send, recv_sem=recv,
            device_id={"fsdp": f, "expert": ex if e is None else e}, device_id_type=MESH)

    def go(copy):
        copy.start()
        pending.append(copy)

    barrier = pltpu.get_barrier_semaphore()
    friends = [partner, y_peer] + near + far + cross
    for k in range(1, EXP):
        e = lax.rem(ex + k, EXP)
        for f in (me, partner):
            pl.semaphore_signal(barrier, inc=1, device_id={"fsdp": f, "expert": e}, device_id_type=MESH)
    for f in friends:
        pl.semaphore_signal(barrier, inc=1, device_id={"fsdp": f, "expert": ex}, device_id_type=MESH)

    feat_in = [pltpu.make_async_copy(src, feats.at[i], in_sem.at[i]) for i, src in enumerate((tok_ref, grd_ref))]
    w_in = [
        pltpu.make_async_copy(src, weights.at[i, pl.ds(0, D_DEV)], in_sem.at[2 + i])
        for i, src in enumerate((wg_ref, wu_ref, wd_ref))]
    for copy in feat_in + w_in:
        copy.start()

    table = one_hot(slots_ref)
    for i in range(2):
        feat_in[i].wait()
        sent[:, i] = pad_features(dot(table, feats[i], NT)).reshape(EXP, SLOT, KPAD).astype(BF16)
    pad = jnp.zeros((KPAD - D_DEV, FF), BF16)
    for i in range(3):
        weights[i, D_DEV:KPAD] = pad
        weights[i, KPAD + D_DEV:2 * KPAD] = pad
        w_in[i].wait()

    pl.semaphore_wait(barrier, len(friends) + 2 * (EXP - 1))

    def peer_expert(k):
        return lax.rem(ex + k, EXP)

    half = ex // 4
    other_copies = [
        remote(sent.at[e], other.at[ex], other_send.at[e], other_recv.at[ex], partner, e)
        for e in (peer_expert(k) for k in range(EXP))]

    @pl.when(half != core)
    def _():
        for copy in other_copies:
            copy.start()

    for k in range(1, EXP):
        e = peer_expert(k)
        go(remote(sent.at[e], mine.at[ex], mine_send.at[e], mine_recv.at[ex], me, e))
    w_copies = [
        remote(weights.at[i, pl.ds(0, D_DEV)], weights.at[i, pl.ds(KPAD, D_DEV)], w_send.at[i], w_recv.at[i], partner)
        for i in range(3)]
    for copy in w_copies:
        go(copy)
    mine[ex] = sent[ex]
    for copy in w_copies:
        copy.wait_recv()
    for k in range(4):
        e = 4 * core + k
        remote(sent.at[e], other.at[e], other_send.at[e], other_recv.at[e], partner, e).wait_recv()
    for k in range(1, EXP):
        e = peer_expert(k)
        remote(sent.at[e], mine.at[e], mine_send.at[e], mine_recv.at[e], me, e).wait_recv()

    own_rows = [
        jnp.concatenate([
            mine[pl.ds(4 * core, 4), i].astype(F32).reshape(HALF, KPAD),
            other[pl.ds(4 * core, 4), i].astype(F32).reshape(HALF, KPAD),
        ], axis=1).astype(BF16)
        for i in range(2)
    ]
    for c in range(NC):
        for i in range(3):
            out = dot(own_rows[i // 2], weights[i, :, c * COLS:(c + 1) * COLS])
            for r in range(4):
                for g in range(3):
                    part[r * NC + c, g * 3 + i] = out[r * SLOT + g * 8:r * SLOT + g * 8 + 8]

    subs = [(q, pl.ds(q, SUB)) for q in range(0, 9, SUB)]

    def up_copy(a, q, block, src, skip=False):
        return remote(src, up_in.at[a - 1, block], up_send.at[a - 1, q], up_recv.at[a - 1, q], far[0] if skip else near[0])

    def down_copy(a, q, block, src):
        return remote(src, down_in.at[a - 1, block], down_send.at[a - 1, q], down_recv.at[a - 1, q], near[1])

    def fin_copy(way, other_plane, q, block, src):
        f = (cross if other_plane else near)[way]
        return remote(src, fin_in.at[way, other_plane, block], fin_send.at[way, other_plane, q],
                      fin_recv.at[way, other_plane, q], f)

    def own_copy(q, block):
        return remote(part.at[z, block], own_in.at[block], own_send.at[q], own_recv.at[q], y_peer)

    for q, block in subs:
        up_copy(8, q, block, part.at[wrap(z + 8 * d), block], True).start()
        up_copy(7, q, block, part.at[wrap(z + 7 * d), block]).start()
        down_copy(7, q, block, part.at[wrap(z - 7 * d), block]).start()
    for q, block in subs:
        own_copy(q, block).start()

    for i in range(2):
        rows_t[i] = mine[:, i].astype(F32).reshape(ROWS, KPAD).T.astype(BF16)
    rows_out = pltpu.make_async_copy(rows_t, rows_ref, out_sem.at[0])
    rows_out.start()

    def up_add(j, q, block):
        up_copy(j + 1, q, block, up_in.at[j, block]).wait_recv()
        up_in[j, block] = up_in[j, block] + part[wrap(z + d * j), block]

    def down_add(j, q, block):
        down_copy(j + 1, q, block, down_in.at[j, block]).wait_recv()
        down_in[j, block] = down_in[j, block] + part[wrap(z - d * j), block]

    for q, block in subs:
        down_add(6, q, block)
        down_copy(6, q, block, down_in.at[6, block]).start()
        up_copy(8, q, block, up_in.at[7, block], True).wait_recv()
        up_add(6, q, block)
        up_in[6, block] = up_in[6, block] + up_in[7, block]
        up_copy(6, q, block, up_in.at[6, block]).start()

    def ring_step(t, _):
        j = 5 - t
        for q, block in subs:
            down_add(j, q, block)
            down_copy(j, q, block, down_in.at[j, block]).start()
            up_add(j, q, block)
            up_copy(j, q, block, up_in.at[j, block]).start()
        return 0

    lax.fori_loop(0, 4, ring_step, 0)
    for q, block in subs:
        down_add(1, q, block)
        for other_plane in (1, 0):
            fin_copy(1, other_plane, q, block, down_in.at[1, block]).start()
        up_add(1, q, block)
        for other_plane in (1, 0):
            fin_copy(0, other_plane, q, block, up_in.at[1, block]).start()

    source = 4 * core + z // NC
    k8 = lax.broadcasted_iota(jnp.int32, (8, 1), 0)
    lane = lax.broadcasted_iota(jnp.int32, (8, ROWS), 1)
    count = jnp.sum(jnp.where(lax.broadcasted_iota(jnp.int32, (1, EXP), 1) == source, counts_ref[...].astype(F32), 0.0),
                    axis=1, keepdims=True)
    spot = lax.broadcasted_iota(jnp.int32, (8, 128), 1)

    def ag_copy(way, a, g, two):
        owner = wrap(z - sign[way] * a)
        return remote(act.at[core, owner, g], act.at[core, owner, g], ag_send.at[way, a + (2 if two else 1) - 1, g],
                      ag_recv.at[owner, g], (far if two else near)[way])

    def ag_arrival(way, a, g):
        owner = wrap(z - sign[way] * a)
        return remote(act.at[core, owner, g], act.at[core, owner, g], ag_send.at[way, 0, g], ag_recv.at[owner, g], near[way])

    def pair_copy(half, owner, g):
        return remote(act.at[half, owner, g], act.at[half, owner, g], pair_send.at[owner, g], pair_recv.at[owner, g], partner)

    def pr_copy(way, a, two):
        owner = wrap(z - sign[way] * a)
        return remote(prob.at[owner], prob.at[owner], pr_send.at[way, a + (2 if two else 1) - 1], pr_recv.at[owner],
                      (far if two else near)[way])

    last = (8, 7)

    def hand_on(a, g):
        for two in (True, False):
            for way in range(2):
                if a + (2 if two else 1) <= last[way]:
                    go(ag_copy(way, a, g, two))

    tile = jnp.zeros((8, 128), F32)
    for g in range(3):
        sums = []
        for i in range(3):
            q = (g * 3 + i) // SUB * SUB
            block = pl.ds(q, SUB)
            if (g * 3 + i) % SUB == 0:
                own_copy(q, block).wait_recv()
                for way in range(2):
                    for other_plane in range(2):
                        fin_copy(way, other_plane, q, block, fin_in.at[way, other_plane, block]).wait_recv()
            n = g * 3 + i
            here = (fin_in[0, 0, n] + fin_in[1, 0, n]) + part[z, n]
            there = (fin_in[0, 1, n] + fin_in[1, 1, n]) + own_in[n]
            sums.append(here + there)
        gate, up, down = sums
        slot = k8 + 8 * g
        live = (slot.astype(F32) < count).astype(F32)
        scale = live * jnp.sum(jnp.where(lane == slot + SLOT * source, prob_ref[...], 0.0), axis=1, keepdims=True)
        sigmoid = jax.nn.sigmoid(gate)
        silu = gate * sigmoid
        hidden = (silu * up).astype(BF16).astype(F32)
        hidden_grad = down * scale
        act[core, z, g, 0] = (hidden_grad * up * sigmoid * (1.0 + gate * (1.0 - sigmoid))).astype(BF16)
        act[core, z, g, 1] = (hidden_grad * silu).astype(BF16)
        act[core, z, g, 2] = (hidden * scale).astype(BF16)
        hand_on(0, g)
        go(pair_copy(core, z, g))
        tile += jnp.where(spot == g, live * jnp.sum(hidden * down, axis=1, keepdims=True), 0.0)
    prob[z] = tile
    for way in range(2):
        for two in (True, False):
            go(pr_copy(way, 0, two))

    for t in range(1, 5):
        for g in range(3):
            for way in range(2):
                if 2 * t <= last[way]:
                    ag_arrival(way, 2 * t, g).wait_recv()
            hand_on(2 * t, g)
            for way in range(2):
                if 2 * t <= last[way]:
                    go(pair_copy(core, wrap(z - sign[way] * 2 * t), g))
        for g in range(3):
            for way in range(2):
                ag_arrival(way, 2 * t - 1, g).wait_recv()
                go(pair_copy(core, wrap(z - sign[way] * (2 * t - 1)), g))
        if t == 1:
            for way in range(2):
                pr_copy(way, 2, False).wait_recv()
                go(pr_copy(way, 2, False))
                pr_copy(way, 1, False).wait_recv()
        if t == 2:
            for way in range(2):
                pr_copy(way, 3, False).wait_recv()
            group = z // NC
            prob_out[...] = sum(prob[group * NC + c] for c in range(NC))
            pp = remote(prob_out, prob_in, pp_send, pp_recv, partner)
            go(pp)

    def pair_wait(owner, _):
        for g in range(3):
            pair_copy(1 - core, owner, g).wait_recv()
        return 0

    lax.fori_loop(0, Z, pair_wait, 0)

    slot_grad = jnp.zeros((ROWS, D_DEV), F32)
    for c in range(NC):
        cols = slice(c * COLS, (c + 1) * COLS)
        for i in range(3):
            full = jnp.concatenate(
                [act[h, r * NC + c, g, i].astype(F32) for h in range(2) for r in range(4) for g in range(3)],
                axis=0).astype(BF16)
            acts[i, :, cols] = full
            if i < 2:
                slot_grad += dot(full, weights[i, 0:D_DEV, cols], NT)
    back_out[...] = pad_features(slot_grad).reshape(EXP, SLOT, KPAD).astype(BF16)
    for k in range(1, EXP):
        e = peer_expert(k)
        go(remote(back_out.at[e], back_in.at[ex], back_send.at[e], back_recv.at[ex], me, e))
    acts_out = pltpu.make_async_copy(acts, acts_ref, out_sem.at[1])
    acts_out.start()
    back_in[ex] = back_out[ex]

    pp.wait_recv()
    total = jnp.where(core == y, prob_out[...], prob_in[...])
    place = lax.broadcasted_iota(jnp.int32, (8, 128), 0) + 8 * spot
    first = 3 * (lax.rem(z, NC) * 2 + core)
    picked = [jnp.sum(jnp.where(place == first + j, total, 0.0), axis=(0, 1), keepdims=True) for j in range(3)]
    pg_ref[...] = jnp.concatenate(picked, axis=1)

    for copy in pending:
        copy.wait_send()

    @pl.when(half != core)
    def _():
        for copy in other_copies:
            copy.wait_send()

    def drain(a, _):
        for q, block in subs:
            up_copy(a, q, block, up_in.at[a - 1, block]).wait_send()
            down_copy(a, q, block, down_in.at[a - 1, block]).wait_send()
        return 0

    lax.fori_loop(2, 8, drain, 0)
    for q, block in subs:
        up_copy(8, q, block, up_in.at[7, block], True).wait_send()
        own_copy(q, block).wait_send()
        for way in range(2):
            for other_plane in range(2):
                fin_copy(way, other_plane, q, block, fin_in.at[way, other_plane, block]).wait_send()
    for k in range(1, EXP):
        e = peer_expert(k)
        remote(back_out.at[e], back_in.at[e], back_send.at[e], back_recv.at[e], me, e).wait_recv()
    back_out_copy = pltpu.make_async_copy(back_in, back_ref, out_sem.at[2])
    back_out_copy.start()
    rows_out.wait()
    acts_out.wait()
    back_out_copy.wait()


def last_kernel(slots_ref, acts_ref, rows_ref, back_ref, tg_ref, *refs):
    grad_refs, (acts, rows, back, tg, grads, in_sem, out_sem) = refs[:3], refs[3:]
    loads = [pltpu.make_async_copy(rows_ref, rows, in_sem.at[0])]
    loads += [pltpu.make_async_copy(acts_ref.at[i], acts.at[i], in_sem.at[1 + i]) for i in range(3)]
    loads += [pltpu.make_async_copy(back_ref, back, in_sem.at[4])]
    for copy in loads:
        copy.start()
    stores = [pltpu.make_async_copy(grads.at[i], grad_refs[i].at[0], out_sem.at[i]) for i in range(3)]
    stores += [pltpu.make_async_copy(tg, tg_ref, out_sem.at[3])]
    table = one_hot(slots_ref)
    loads[0].wait()
    for i in range(3):
        loads[1 + i].wait()
        grads[i] = dot(rows[i // 2], acts[i])[:D_DEV]
        stores[i].start()
    loads[4].wait()
    back_t = back[...].astype(F32).reshape(ROWS, KPAD).T.astype(BF16)
    tg[...] = dot(back_t, table)[:D_DEV].astype(BF16)
    stores[3].start()
    for copy in stores:
        copy.wait()


def local(tokens, out_grad, slot_rows, expert_counts, route_prob, w_gate, w_up, w_down):
    vmem = pl.BlockSpec(memory_space=pltpu.VMEM)
    hbm = pl.BlockSpec(memory_space=pl.ANY)
    dma = pltpu.SemaphoreType.DMA
    shape = jax.ShapeDtypeStruct
    acts, rows, back, pg = pl.pallas_call(
        kernel,
        out_shape=(shape((3, ROWS, FF), BF16), shape((2, KPAD, ROWS), BF16), shape((EXP, SLOT, KPAD), BF16), shape((1, 3), F32)),
        in_specs=[vmem] * 3 + [hbm] * 5,
        out_specs=(hbm, hbm, hbm, vmem),
        scratch_shapes=[
            pltpu.VMEM((2, D_DEV, TOK), BF16),
            pltpu.VMEM((EXP, 2, SLOT, KPAD), BF16),
            pltpu.VMEM((EXP, 2, SLOT, KPAD), BF16),
            pltpu.VMEM((EXP, 2, SLOT, KPAD), BF16),
            pltpu.VMEM((3, 2 * KPAD, FF), BF16),
            pltpu.VMEM((Z, 9, 8, COLS), F32),
            pltpu.VMEM((8, 9, 8, COLS), F32),
            pltpu.VMEM((7, 9, 8, COLS), F32),
            pltpu.VMEM((2, 2, 9, 8, COLS), F32),
            pltpu.VMEM((9, 8, COLS), F32),
            pltpu.VMEM((2, Z, 3, 3, 8, COLS), BF16),
            pltpu.VMEM((3, ROWS, FF), BF16),
            pltpu.VMEM((2, KPAD, ROWS), BF16),
            pltpu.VMEM((Z, 8, 128), F32),
            pltpu.VMEM((8, 128), F32),
            pltpu.VMEM((8, 128), F32),
            pltpu.VMEM((EXP, SLOT, KPAD), BF16),
            pltpu.VMEM((EXP, SLOT, KPAD), BF16),
            dma((EXP,)), dma((EXP,)), dma((EXP,)), dma((EXP,)), dma((3,)), dma((3,)),
            dma((8, 9)), dma((8, 9)), dma((7, 9)), dma((7, 9)), dma((2, 2, 9)), dma((2, 2, 9)), dma((9,)), dma((9,)),
            dma((2, 8, 3)), dma((Z, 3)), dma((Z, 3)), dma((Z, 3)), dma((2, 3)), dma((Z,)), dma, dma,
            dma((EXP,)), dma((EXP,)), dma((5,)), dma((3,)),
        ],
        compiler_params=pltpu.CompilerParams(collective_id=0, has_side_effects=True),
    )(slot_rows, route_prob, expert_counts, tokens.T, out_grad.T, w_gate[0], w_up[0], w_down[0])
    grad = shape((1, D_DEV, FF), F32)
    tg, gg, ug, dg = pl.pallas_call(
        last_kernel,
        out_shape=(shape((D_DEV, TOK), BF16), grad, grad, grad),
        in_specs=[vmem, hbm, hbm, hbm],
        out_specs=(hbm,) * 4,
        scratch_shapes=[
            pltpu.VMEM((3, ROWS, FF), BF16),
            pltpu.VMEM((2, KPAD, ROWS), BF16),
            pltpu.VMEM((EXP, SLOT, KPAD), BF16),
            pltpu.VMEM((D_DEV, TOK), BF16),
            pltpu.VMEM((3, D_DEV, FF), F32),
            dma((5,)), dma((4,)),
        ],
    )(slot_rows, acts, rows, back)
    return tg.T, gg, ug, dg, pg


def solution(mesh):
    return jax.shard_map(
        local,
        mesh=mesh,
        in_specs=(
            P("expert", "fsdp"),
            P("expert", "fsdp"),
            P("expert", None, None),
            P("expert", None),
            P("expert", None),
            P("expert", "fsdp", None),
            P("expert", "fsdp", None),
            P("expert", "fsdp", None),
        ),
        out_specs=(
            P("expert", "fsdp"),
            P("expert", "fsdp", None),
            P("expert", "fsdp", None),
            P("expert", "fsdp", None),
            P("expert", "fsdp"),
        ),
        check_vma=False,
    )
```

```python
import jax
import jax.numpy as jnp
from jax import lax
from jax.experimental import pallas as pl
from jax.experimental.pallas import tpu as pltpu
from jax.sharding import PartitionSpec as P

MESH = pl.DeviceIdType.MESH
F32, BF16 = jnp.float32, jnp.bfloat16

Z = 16
EXP = 8
SLOT = 24
ROWS = EXP * SLOT
HALF = ROWS // 2
D_DEV = 80
KPAD = 128
FF = 1536
COLS = 384
NC = FF // COLS
TOK = 1024
SUB = 1
NT = (((1,), (1,)), ((), ()))


def dot(a, b, dims=(((1,), (0,)), ((), ()))):
    return lax.dot_general(a, b, dims, preferred_element_type=F32)


def slot_column(slots_ref):
    wide = jnp.concatenate([slots_ref[0].astype(F32), jnp.zeros((EXP, KPAD - SLOT), F32)], axis=1)
    tall = wide.T
    return jnp.concatenate([tall[:SLOT, e:e + 1] for e in range(EXP)], axis=0)


def one_hot(slots_ref):
    columns = lax.broadcasted_iota(jnp.int32, (ROWS, TOK), 1)
    return jnp.where(slot_column(slots_ref) == columns.astype(F32), 1.0, 0.0).astype(BF16)


def pad_features(rows):
    return jnp.concatenate([rows, jnp.zeros((ROWS, KPAD - D_DEV), F32)], axis=1)


def kernel(
    slots_ref, prob_ref, counts_ref, tok_ref, grd_ref, wg_ref, wu_ref, wd_ref,
    acts_ref, rows_ref, back_ref, pg_ref,
    feats, sent, mine, other, weights, part, up_in, down_in, fin_in, own_in, act,
    prob, prob_out, prob_in, back_out, back_in,
    mine_send, mine_recv, other_send, other_recv, w_send, w_recv,
    up_send, up_recv, down_send, down_recv, fin_send, fin_recv, own_send, own_recv,
    ag_send, ag_recv, pair_send, pair_recv, pr_send, pr_recv, pp_send, pp_recv, back_send, back_recv, in_sem,
):
    me = lax.axis_index("fsdp")
    ex = lax.axis_index("expert")
    core = lax.rem(me, 2)
    z = lax.rem(me // 2, Z)
    y = me // (2 * Z)
    d = 1 - 2 * core
    partner = me + d

    def at_z(pos, plane=None):
        return ((y if plane is None else plane) * Z + pos) * 2 + core

    def wrap(pos):
        return lax.rem(pos + 2 * Z, Z)

    near = [at_z(wrap(z + d)), at_z(wrap(z - d))]
    far = [at_z(wrap(z + 2 * d)), at_z(wrap(z - 2 * d))]
    cross = [at_z(wrap(z + d), 1 - y), at_z(wrap(z - d), 1 - y)]
    y_peer = at_z(z, 1 - y)
    sign = (d, -d)
    def remote(src, dst, send, recv, f, e=None):
        return pltpu.make_async_remote_copy(
            src_ref=src, dst_ref=dst, send_sem=send, recv_sem=recv,
            device_id={"fsdp": f, "expert": ex if e is None else e}, device_id_type=MESH)

    def sent_all(ref, sem):
        remote(ref, ref, sem, sem, partner).wait_send()

    barrier = pltpu.get_barrier_semaphore()
    friends = [partner, y_peer] + near + far + cross
    for k in range(1, EXP):
        e = lax.rem(ex + k, EXP)
        for f in (me, partner):
            pl.semaphore_signal(barrier, inc=1, device_id={"fsdp": f, "expert": e}, device_id_type=MESH)
    for f in friends:
        pl.semaphore_signal(barrier, inc=1, device_id={"fsdp": f, "expert": ex}, device_id_type=MESH)

    feat_in = [pltpu.make_async_copy(src, feats.at[i], in_sem.at[i]) for i, src in enumerate((tok_ref, grd_ref))]
    w_in = [
        pltpu.make_async_copy(src, weights.at[i, pl.ds(0, D_DEV)], in_sem.at[2 + i])
        for i, src in enumerate((wg_ref, wu_ref, wd_ref))]
    for copy in feat_in + w_in:
        copy.start()

    table = one_hot(slots_ref)
    for i in range(2):
        feat_in[i].wait()
        sent[:, i] = pad_features(dot(table, feats[i], NT)).reshape(EXP, SLOT, KPAD).astype(BF16)
    pad = jnp.zeros((KPAD - D_DEV, FF), BF16)
    for i in range(3):
        weights[i, D_DEV:KPAD] = pad
        weights[i, KPAD + D_DEV:2 * KPAD] = pad
        w_in[i].wait()

    pl.semaphore_wait(barrier, len(friends) + 2 * (EXP - 1))

    def peer_expert(k):
        return lax.rem(ex + k, EXP)

    half = ex // 4
    other_copies = [
        remote(sent.at[e], other.at[ex], other_send, other_recv.at[ex], partner, e)
        for e in (peer_expert(k) for k in range(EXP))]

    @pl.when(half != core)
    def _():
        for copy in other_copies:
            copy.start()

    mine_copies = [
        remote(sent.at[e], mine.at[ex], mine_send, mine_recv.at[ex], me, e)
        for e in (peer_expert(k) for k in range(1, EXP))]

    @pl.when(half == core)
    def _():
        for copy in mine_copies:
            copy.start()

    w_copies = [
        remote(weights.at[i, pl.ds(0, D_DEV)], weights.at[i, pl.ds(KPAD, D_DEV)], w_send, w_recv.at[i], partner)
        for i in range(3)]
    for copy in w_copies:
        copy.start()
    mine[ex] = sent[ex]
    for copy in w_copies:
        copy.wait_recv()

    def mine_wait(e):
        @pl.when(e != ex)
        def _():
            remote(sent.at[e], mine.at[e], mine_send, mine_recv.at[e], me, e).wait_recv()

    for k in range(4):
        e = 4 * core + k
        remote(sent.at[e], other.at[e], other_send, other_recv.at[e], partner, e).wait_recv()
        mine_wait(e)

    @pl.when(half != core)
    def _():
        for copy in mine_copies:
            copy.start()

    own_rows = [
        jnp.concatenate([
            mine[pl.ds(4 * core, 4), i].astype(F32).reshape(HALF, KPAD),
            other[pl.ds(4 * core, 4), i].astype(F32).reshape(HALF, KPAD),
        ], axis=1).astype(BF16)
        for i in range(2)
    ]
    for c in range(NC):
        for i in range(3):
            out = dot(own_rows[i // 2], weights[i, :, c * COLS:(c + 1) * COLS])
            for r in range(4):
                for g in range(3):
                    part[r * NC + c, g * 3 + i] = out[r * SLOT + g * 8:r * SLOT + g * 8 + 8]

    subs = [(q, pl.ds(q, SUB)) for q in range(0, 9, SUB)]

    def up_copy(a, q, block, src, skip=False):
        return remote(src, up_in.at[a - 1, block], up_send, up_recv.at[a - 1, q], far[0] if skip else near[0])

    def down_copy(a, q, block, src):
        return remote(src, down_in.at[a - 1, block], down_send, down_recv.at[a - 1, q], near[1])

    def fin_copy(way, other_plane, q, block, src):
        f = (cross if other_plane else near)[way]
        return remote(src, fin_in.at[way, other_plane, block], fin_send,
                      fin_recv.at[way, other_plane, q], f)

    def own_copy(q, block):
        return remote(part.at[z, block], own_in.at[block], own_send, own_recv.at[q], y_peer)

    for q, block in subs:
        up_copy(8, q, block, part.at[wrap(z + 8 * d), block], True).start()
        up_copy(7, q, block, part.at[wrap(z + 7 * d), block]).start()
        down_copy(7, q, block, part.at[wrap(z - 7 * d), block]).start()
    for q, block in subs:
        own_copy(q, block).start()

    for k in range(4):
        mine_wait(4 * (1 - core) + k)
    for i in range(2):
        rows_ref[i] = mine[:, i].astype(F32).reshape(ROWS, KPAD).T.astype(BF16)

    def up_add(j, q, block):
        up_copy(j + 1, q, block, up_in.at[j, block]).wait_recv()
        up_in[j, block] = up_in[j, block] + part[wrap(z + d * j), block]

    def down_add(j, q, block):
        down_copy(j + 1, q, block, down_in.at[j, block]).wait_recv()
        down_in[j, block] = down_in[j, block] + part[wrap(z - d * j), block]

    for q, block in subs:
        down_add(6, q, block)
        down_copy(6, q, block, down_in.at[6, block]).start()
        up_copy(8, q, block, up_in.at[7, block], True).wait_recv()
        up_add(6, q, block)
        up_in[6, block] = up_in[6, block] + up_in[7, block]
        up_copy(6, q, block, up_in.at[6, block]).start()

    def ring_step(t, _):
        j = 5 - t
        for q, block in subs:
            down_add(j, q, block)
            down_copy(j, q, block, down_in.at[j, block]).start()
            up_add(j, q, block)
            up_copy(j, q, block, up_in.at[j, block]).start()
        return 0

    lax.fori_loop(0, 4, ring_step, 0)
    for q, block in subs:
        down_add(1, q, block)
        for other_plane in (1, 0):
            fin_copy(1, other_plane, q, block, down_in.at[1, block]).start()
        up_add(1, q, block)
        for other_plane in (1, 0):
            fin_copy(0, other_plane, q, block, up_in.at[1, block]).start()

    source = 4 * core + z // NC
    k8 = lax.broadcasted_iota(jnp.int32, (8, 1), 0)
    lane = lax.broadcasted_iota(jnp.int32, (8, ROWS), 1)
    count = jnp.sum(jnp.where(lax.broadcasted_iota(jnp.int32, (1, EXP), 1) == source, counts_ref[...].astype(F32), 0.0),
                    axis=1, keepdims=True)
    spot = lax.broadcasted_iota(jnp.int32, (8, 128), 1)

    def ag_copy(way, a, g, two):
        owner = wrap(z - sign[way] * a)
        return remote(act.at[core, owner, g], act.at[core, owner, g], ag_send,
                      ag_recv.at[owner, g], (far if two else near)[way])

    def ag_arrival(way, a, g):
        owner = wrap(z - sign[way] * a)
        return remote(act.at[core, owner, g], act.at[core, owner, g], ag_send, ag_recv.at[owner, g], near[way])

    def pair_copy(owner, g):
        return remote(act.at[core, owner, g], act.at[core, owner, g], pair_send, pair_recv, partner)

    def pr_copy(way, a, two):
        owner = wrap(z - sign[way] * a)
        return remote(prob.at[owner], prob.at[owner], pr_send, pr_recv.at[owner],
                      (far if two else near)[way])

    last = (8, 7)

    def hand_on(a, g):
        for two in (True, False):
            for way in range(2):
                if a + (2 if two else 1) <= last[way]:
                    ag_copy(way, a, g, two).start()

    tile = jnp.zeros((8, 128), F32)
    for g in range(3):
        sums = []
        for i in range(3):
            q = (g * 3 + i) // SUB * SUB
            block = pl.ds(q, SUB)
            if (g * 3 + i) % SUB == 0:
                own_copy(q, block).wait_recv()
                for way in range(2):
                    for other_plane in range(2):
                        fin_copy(way, other_plane, q, block, fin_in.at[way, other_plane, block]).wait_recv()
            n = g * 3 + i
            here = (fin_in[0, 0, n] + fin_in[1, 0, n]) + part[z, n]
            there = (fin_in[0, 1, n] + fin_in[1, 1, n]) + own_in[n]
            sums.append(here + there)
        gate, up, down = sums
        slot = k8 + 8 * g
        live = (slot.astype(F32) < count).astype(F32)
        scale = live * jnp.sum(jnp.where(lane == slot + SLOT * source, prob_ref[...], 0.0), axis=1, keepdims=True)
        sigmoid = jax.nn.sigmoid(gate)
        silu = gate * sigmoid
        hidden = (silu * up).astype(BF16).astype(F32)
        hidden_grad = down * scale
        act[core, z, g, 0] = (hidden_grad * up * sigmoid * (1.0 + gate * (1.0 - sigmoid))).astype(BF16)
        act[core, z, g, 1] = (hidden_grad * silu).astype(BF16)
        act[core, z, g, 2] = (hidden * scale).astype(BF16)
        hand_on(0, g)
        pair_copy(z, g).start()
        tile += jnp.where(spot == g, live * jnp.sum(hidden * down, axis=1, keepdims=True), 0.0)
    prob[z] = tile
    for way in range(2):
        for two in (True, False):
            pr_copy(way, 0, two).start()

    for t in range(1, 5):
        for g in range(3):
            for way in range(2):
                if 2 * t <= last[way]:
                    ag_arrival(way, 2 * t, g).wait_recv()
            hand_on(2 * t, g)
            for way in range(2):
                if 2 * t <= last[way]:
                    pair_copy(wrap(z - sign[way] * 2 * t), g).start()
        for g in range(3):
            for way in range(2):
                ag_arrival(way, 2 * t - 1, g).wait_recv()
                pair_copy(wrap(z - sign[way] * (2 * t - 1)), g).start()
        if t == 1:
            sent_all(part.at[pl.ds(0, 7)], up_send)
            sent_all(part.at[pl.ds(0, 6)], down_send)
            sent_all(part.at[pl.ds(0, 4)], fin_send)
            sent_all(part.at[0], own_send)
            sent_all(sent.at[pl.ds(0, EXP - 1)], mine_send)
            sent_all(weights.at[pl.ds(0, 3), pl.ds(0, D_DEV)], w_send)

            @pl.when(half != core)
            def _():
                sent_all(sent, other_send)

            for way in range(2):
                pr_copy(way, 2, False).wait_recv()
                pr_copy(way, 2, False).start()
                pr_copy(way, 1, False).wait_recv()
        if t == 2:
            for way in range(2):
                pr_copy(way, 3, False).wait_recv()
            group = z // NC
            prob_out[...] = sum(prob[group * NC + c] for c in range(NC))
            pp = remote(prob_out, prob_in, pp_send, pp_recv, partner)
            pp.start()

    remote(act.at[1 - core], act.at[1 - core], pair_send, pair_recv, partner).wait_recv()

    slot_grad = jnp.zeros((ROWS, D_DEV), F32)
    for c in range(NC):
        cols = slice(c * COLS, (c + 1) * COLS)
        for i in range(3):
            full = jnp.concatenate(
                [act[h, r * NC + c, g, i].astype(F32) for h in range(2) for r in range(4) for g in range(3)],
                axis=0).astype(BF16)
            acts_ref[i, :, cols] = full
            if i < 2:
                slot_grad += dot(full, weights[i, 0:D_DEV, cols], NT)
    back_out[...] = pad_features(slot_grad).reshape(EXP, SLOT, KPAD).astype(BF16)
    for k in range(1, EXP):
        e = peer_expert(k)
        remote(back_out.at[e], back_in.at[ex], back_send, back_recv.at[ex], me, e).start()
    back_in[ex] = back_out[ex]

    pp.wait_recv()
    total = jnp.where(core == y, prob_out[...], prob_in[...])
    place = lax.broadcasted_iota(jnp.int32, (8, 128), 0) + 8 * spot
    first = 3 * (lax.rem(z, NC) * 2 + core)
    picked = [jnp.sum(jnp.where(place == first + j, total, 0.0), axis=(0, 1), keepdims=True) for j in range(3)]
    pg_ref[...] = jnp.concatenate(picked, axis=1)

    sent_all(act.at[core, pl.ds(0, 15)], ag_send)
    sent_all(act.at[core], pair_send)
    sent_all(prob.at[pl.ds(0, 6)], pr_send)
    sent_all(prob_out, pp_send)
    sent_all(back_out.at[pl.ds(0, EXP - 1)], back_send)
    for k in range(1, EXP):
        e = peer_expert(k)
        remote(back_out.at[e], back_in.at[e], back_send, back_recv.at[e], me, e).wait_recv()
    back_ref[...] = back_in[...]


def last_kernel(slots_ref, acts_ref, rows_ref, back_ref, pg_in, tg_ref, gg_ref, ug_ref, dg_ref, pg_ref, tg, grads, out_sem):
    grad_refs = (gg_ref, ug_ref, dg_ref)
    stores = [pltpu.make_async_copy(grads.at[i], grad_refs[i].at[0], out_sem.at[i]) for i in range(3)]
    stores += [pltpu.make_async_copy(tg, tg_ref, out_sem.at[3])]
    for i in range(3):
        grads[i] = dot(rows_ref[i // 2], acts_ref[i])[:D_DEV]
        stores[i].start()
    pg_ref[...] = pg_in[...]
    back_t = back_ref[...].astype(F32).reshape(ROWS, KPAD).T.astype(BF16)
    tg[...] = dot(back_t, one_hot(slots_ref))[:D_DEV].astype(BF16)
    stores[3].start()
    for copy in stores:
        copy.wait()


def local(tokens, out_grad, slot_rows, expert_counts, route_prob, w_gate, w_up, w_down):
    vmem = pl.BlockSpec(memory_space=pltpu.VMEM)
    hbm = pl.BlockSpec(memory_space=pl.ANY)
    dma = pltpu.SemaphoreType.DMA
    shape = jax.ShapeDtypeStruct
    acts, rows, back, pg = pl.pallas_call(
        kernel,
        out_shape=(
            pltpu.VMEM((3, ROWS, FF), BF16), pltpu.VMEM((2, KPAD, ROWS), BF16), pltpu.VMEM((EXP, SLOT, KPAD), BF16),
            pltpu.VMEM((1, 3), F32)),
        in_specs=[vmem] * 3 + [hbm] * 5,
        out_specs=(vmem,) * 4,
        scratch_shapes=[
            pltpu.VMEM((2, D_DEV, TOK), BF16),
            pltpu.VMEM((EXP, 2, SLOT, KPAD), BF16),
            pltpu.VMEM((EXP, 2, SLOT, KPAD), BF16),
            pltpu.VMEM((EXP, 2, SLOT, KPAD), BF16),
            pltpu.VMEM((3, 2 * KPAD, FF), BF16),
            pltpu.VMEM((Z, 9, 8, COLS), F32),
            pltpu.VMEM((8, 9, 8, COLS), F32),
            pltpu.VMEM((7, 9, 8, COLS), F32),
            pltpu.VMEM((2, 2, 9, 8, COLS), F32),
            pltpu.VMEM((9, 8, COLS), F32),
            pltpu.VMEM((2, Z, 3, 3, 8, COLS), BF16),
            pltpu.VMEM((Z, 8, 128), F32),
            pltpu.VMEM((8, 128), F32),
            pltpu.VMEM((8, 128), F32),
            pltpu.VMEM((EXP, SLOT, KPAD), BF16),
            pltpu.VMEM((EXP, SLOT, KPAD), BF16),
            dma, dma((EXP,)), dma, dma((EXP,)), dma, dma((3,)),
            dma, dma((8, 9)), dma, dma((7, 9)), dma, dma((2, 2, 9)), dma, dma((9,)),
            dma, dma((Z, 3)), dma, dma, dma, dma((Z,)), dma, dma, dma, dma((EXP,)), dma((5,)),
        ],
        compiler_params=pltpu.CompilerParams(collective_id=0, has_side_effects=True),
    )(slot_rows, route_prob, expert_counts, tokens.T, out_grad.T, w_gate[0], w_up[0], w_down[0])
    grad = shape((1, D_DEV, FF), F32)
    tg, gg, ug, dg, pg = pl.pallas_call(
        last_kernel,
        out_shape=(shape((D_DEV, TOK), BF16), grad, grad, grad, shape((1, 3), F32)),
        in_specs=[vmem] * 5,
        out_specs=(hbm,) * 4 + (vmem,),
        scratch_shapes=[pltpu.VMEM((D_DEV, TOK), BF16), pltpu.VMEM((3, D_DEV, FF), F32), dma((4,))],
    )(slot_rows, acts, rows, back, pg)
    return tg.T, gg, ug, dg, pg


def solution(mesh):
    return jax.shard_map(
        local,
        mesh=mesh,
        in_specs=(
            P("expert", "fsdp"),
            P("expert", "fsdp"),
            P("expert", None, None),
            P("expert", None),
            P("expert", None),
            P("expert", "fsdp", None),
            P("expert", "fsdp", None),
            P("expert", "fsdp", None),
        ),
        out_specs=(
            P("expert", "fsdp"),
            P("expert", "fsdp", None),
            P("expert", "fsdp", None),
            P("expert", "fsdp", None),
            P("expert", "fsdp"),
        ),
        check_vma=False,
    )
```

```python
import jax
import jax.numpy as jnp
from jax import lax
from jax.experimental import pallas as pl
from jax.experimental.pallas import tpu as pltpu
from jax.sharding import PartitionSpec as P

MESH = pl.DeviceIdType.MESH
F32, BF16 = jnp.float32, jnp.bfloat16

Z = 16
EXP = 8
SLOT = 24
ROWS = EXP * SLOT
HALF = ROWS // 2
D_DEV = 80
KPAD = 128
FF = 1536
COLS = 384
NC = FF // COLS
TOK = 1024
SUB = 1
NT = (((1,), (1,)), ((), ()))


def dot(a, b, dims=(((1,), (0,)), ((), ()))):
    return lax.dot_general(a, b, dims, preferred_element_type=F32)


def slot_column(slots_ref):
    wide = jnp.concatenate([slots_ref[0].astype(F32), jnp.zeros((EXP, KPAD - SLOT), F32)], axis=1)
    tall = wide.T
    return jnp.concatenate([tall[:SLOT, e:e + 1] for e in range(EXP)], axis=0)


def one_hot(slots_ref):
    columns = lax.broadcasted_iota(jnp.int32, (ROWS, TOK), 1)
    return jnp.where(slot_column(slots_ref) == columns.astype(F32), 1.0, 0.0).astype(BF16)


def pad_features(rows):
    return jnp.concatenate([rows, jnp.zeros((ROWS, KPAD - D_DEV), F32)], axis=1)


def kernel(
    slots_ref, prob_ref, counts_ref, tok_ref, grd_ref, wg_ref, wu_ref, wd_ref,
    acts_ref, rows_ref, back_ref, pg_ref,
    feats, sent, mine, other, weights, part, up_in, down_in, fin_in, own_in, act,
    prob, prob_out, prob_in, back_out, back_in,
    mine_send, mine_recv, other_send, other_recv, w_send, w_recv,
    up_send, up_recv, down_send, down_recv, fin_send, fin_recv, own_send, own_recv,
    ag_send, ag_recv, pair_send, pair_recv, pr_send, pr_recv, pp_send, pp_recv, back_send, back_recv, in_sem,
):
    me = lax.axis_index("fsdp")
    ex = lax.axis_index("expert")
    core = lax.rem(me, 2)
    z = lax.rem(me // 2, Z)
    y = me // (2 * Z)
    d = 1 - 2 * core
    partner = me + d

    def at_z(pos, plane=None):
        return ((y if plane is None else plane) * Z + pos) * 2 + core

    def wrap(pos):
        return lax.rem(pos + 2 * Z, Z)

    near = [at_z(wrap(z + d)), at_z(wrap(z - d))]
    far = [at_z(wrap(z + 2 * d)), at_z(wrap(z - 2 * d))]
    cross = [at_z(wrap(z + d), 1 - y), at_z(wrap(z - d), 1 - y)]
    y_peer = at_z(z, 1 - y)
    sign = (d, -d)
    def remote(src, dst, send, recv, f, e=None):
        return pltpu.make_async_remote_copy(
            src_ref=src, dst_ref=dst, send_sem=send, recv_sem=recv,
            device_id={"fsdp": f, "expert": ex if e is None else e}, device_id_type=MESH)

    def sent_all(ref, sem):
        remote(ref, ref, sem, sem, partner).wait_send()

    barrier = pltpu.get_barrier_semaphore()
    friends = [partner, y_peer] + near + far + cross
    for k in range(1, EXP):
        e = lax.rem(ex + k, EXP)
        for f in (me, partner):
            pl.semaphore_signal(barrier, inc=1, device_id={"fsdp": f, "expert": e}, device_id_type=MESH)
    for f in friends:
        pl.semaphore_signal(barrier, inc=1, device_id={"fsdp": f, "expert": ex}, device_id_type=MESH)

    feat_in = [pltpu.make_async_copy(src, feats.at[i], in_sem.at[i]) for i, src in enumerate((tok_ref, grd_ref))]
    w_in = [
        pltpu.make_async_copy(src, weights.at[i, pl.ds(0, D_DEV)], in_sem.at[2 + i])
        for i, src in enumerate((wg_ref, wu_ref, wd_ref))]
    for copy in feat_in + w_in:
        copy.start()

    table = one_hot(slots_ref)
    for i in range(2):
        feat_in[i].wait()
        sent[:, i] = pad_features(dot(table, feats[i], NT)).reshape(EXP, SLOT, KPAD).astype(BF16)
    pad = jnp.zeros((KPAD - D_DEV, FF), BF16)
    for i in range(3):
        weights[i, D_DEV:KPAD] = pad
        weights[i, KPAD + D_DEV:2 * KPAD] = pad
        w_in[i].wait()

    pl.semaphore_wait(barrier, len(friends) + 2 * (EXP - 1))

    def peer_expert(k):
        return lax.rem(ex + k, EXP)

    half = ex // 4
    other_copies = [
        remote(sent.at[e], other.at[ex], other_send, other_recv.at[ex], partner, e)
        for e in (peer_expert(k) for k in range(EXP))]

    @pl.when(half != core)
    def _():
        for copy in other_copies:
            copy.start()

    mine_copies = [
        remote(sent.at[e], mine.at[ex], mine_send, mine_recv.at[ex], me, e)
        for e in (peer_expert(k) for k in range(1, EXP))]

    @pl.when(half == core)
    def _():
        for copy in mine_copies:
            copy.start()

    w_copies = [
        remote(weights.at[i, pl.ds(0, D_DEV)], weights.at[i, pl.ds(KPAD, D_DEV)], w_send, w_recv.at[i], partner)
        for i in range(3)]
    for copy in w_copies:
        copy.start()
    mine[ex] = sent[ex]
    for copy in w_copies:
        copy.wait_recv()

    def mine_wait(e):
        @pl.when(e != ex)
        def _():
            remote(sent.at[e], mine.at[e], mine_send, mine_recv.at[e], me, e).wait_recv()

    for k in range(4):
        e = 4 * core + k
        remote(sent.at[e], other.at[e], other_send, other_recv.at[e], partner, e).wait_recv()
        mine_wait(e)

    @pl.when(half != core)
    def _():
        for copy in mine_copies:
            copy.start()

    own_rows = [
        jnp.concatenate([
            mine[pl.ds(4 * core, 4), i].astype(F32).reshape(HALF, KPAD),
            other[pl.ds(4 * core, 4), i].astype(F32).reshape(HALF, KPAD),
        ], axis=1).astype(BF16)
        for i in range(2)
    ]
    for c in range(NC):
        for i in range(3):
            out = dot(own_rows[i // 2], weights[i, :, c * COLS:(c + 1) * COLS])
            for r in range(4):
                for g in range(3):
                    part[r * NC + c, g * 3 + i] = out[r * SLOT + g * 8:r * SLOT + g * 8 + 8]

    subs = [(q, pl.ds(q, SUB)) for q in range(0, 9, SUB)]

    def up_copy(a, q, block, src, skip=False):
        return remote(src, up_in.at[a - 1, block], up_send, up_recv.at[a - 1, q], far[0] if skip else near[0])

    def down_copy(a, q, block, src):
        return remote(src, down_in.at[a - 1, block], down_send, down_recv.at[a - 1, q], near[1])

    def fin_copy(way, other_plane, q, block, src):
        f = (cross if other_plane else near)[way]
        return remote(src, fin_in.at[way, other_plane, block], fin_send,
                      fin_recv.at[way, other_plane, q], f)

    def own_copy(q, block):
        return remote(part.at[z, block], own_in.at[block], own_send, own_recv.at[q], y_peer)

    for q, block in subs:
        up_copy(8, q, block, part.at[wrap(z + 8 * d), block], True).start()
        up_copy(7, q, block, part.at[wrap(z + 7 * d), block]).start()
        down_copy(7, q, block, part.at[wrap(z - 7 * d), block]).start()
    for q, block in subs:
        own_copy(q, block).start()

    for k in range(4):
        mine_wait(4 * (1 - core) + k)
    for i in range(2):
        rows_ref[i] = mine[:, i].astype(F32).reshape(ROWS, KPAD).T.astype(BF16)

    def up_add(j, q, block):
        up_copy(j + 1, q, block, up_in.at[j, block]).wait_recv()
        up_in[j, block] = up_in[j, block] + part[wrap(z + d * j), block]

    def down_add(j, q, block):
        down_copy(j + 1, q, block, down_in.at[j, block]).wait_recv()
        down_in[j, block] = down_in[j, block] + part[wrap(z - d * j), block]

    for q, block in subs:
        down_add(6, q, block)
        down_copy(6, q, block, down_in.at[6, block]).start()
        up_copy(8, q, block, up_in.at[7, block], True).wait_recv()
        up_add(6, q, block)
        up_in[6, block] = up_in[6, block] + up_in[7, block]
        up_copy(6, q, block, up_in.at[6, block]).start()

    def ring_step(t, _):
        j = 5 - t
        for q, block in subs:
            down_add(j, q, block)
            down_copy(j, q, block, down_in.at[j, block]).start()
            up_add(j, q, block)
            up_copy(j, q, block, up_in.at[j, block]).start()
        return 0

    lax.fori_loop(0, 4, ring_step, 0)
    for q, block in subs:
        down_add(1, q, block)
        for other_plane in (1, 0):
            fin_copy(1, other_plane, q, block, down_in.at[1, block]).start()
        up_add(1, q, block)
        for other_plane in (1, 0):
            fin_copy(0, other_plane, q, block, up_in.at[1, block]).start()

    source = 4 * core + z // NC
    k8 = lax.broadcasted_iota(jnp.int32, (8, 1), 0)
    lane = lax.broadcasted_iota(jnp.int32, (8, ROWS), 1)
    count = jnp.sum(jnp.where(lax.broadcasted_iota(jnp.int32, (1, EXP), 1) == source, counts_ref[...].astype(F32), 0.0),
                    axis=1, keepdims=True)
    spot = lax.broadcasted_iota(jnp.int32, (8, 128), 1)

    def ag_copy(way, a, g, two):
        owner = wrap(z - sign[way] * a)
        return remote(act.at[core, owner, g], act.at[core, owner, g], ag_send,
                      ag_recv.at[owner, g], (far if two else near)[way])

    def ag_arrival(way, a, g):
        owner = wrap(z - sign[way] * a)
        return remote(act.at[core, owner, g], act.at[core, owner, g], ag_send, ag_recv.at[owner, g], near[way])

    def pair_copy(owner, g):
        return remote(act.at[core, owner, g], act.at[core, owner, g], pair_send, pair_recv, partner)

    def pr_copy(way, a, two):
        owner = wrap(z - sign[way] * a)
        return remote(prob.at[owner], prob.at[owner], pr_send, pr_recv.at[owner],
                      (far if two else near)[way])

    last = (8, 7)

    def hand_on(a, g):
        for two in (True, False):
            for way in range(2):
                if a + (2 if two else 1) <= last[way]:
                    ag_copy(way, a, g, two).start()

    tile = jnp.zeros((8, 128), F32)
    for g in range(3):
        sums = []
        for i in range(3):
            q = (g * 3 + i) // SUB * SUB
            block = pl.ds(q, SUB)
            if (g * 3 + i) % SUB == 0:
                own_copy(q, block).wait_recv()
                for way in range(2):
                    for other_plane in range(2):
                        fin_copy(way, other_plane, q, block, fin_in.at[way, other_plane, block]).wait_recv()
            n = g * 3 + i
            here = (fin_in[0, 0, n] + fin_in[1, 0, n]) + part[z, n]
            there = (fin_in[0, 1, n] + fin_in[1, 1, n]) + own_in[n]
            sums.append(here + there)
        gate, up, down = sums
        slot = k8 + 8 * g
        live = (slot.astype(F32) < count).astype(F32)
        scale = live * jnp.sum(jnp.where(lane == slot + SLOT * source, prob_ref[...], 0.0), axis=1, keepdims=True)
        sigmoid = jax.nn.sigmoid(gate)
        silu = gate * sigmoid
        hidden = (silu * up).astype(BF16).astype(F32)
        hidden_grad = down * scale
        act[core, z, g, 0] = (hidden_grad * up * sigmoid * (1.0 + gate * (1.0 - sigmoid))).astype(BF16)
        act[core, z, g, 1] = (hidden_grad * silu).astype(BF16)
        act[core, z, g, 2] = (hidden * scale).astype(BF16)
        hand_on(0, g)
        pair_copy(z, g).start()
        tile += jnp.where(spot == g, live * jnp.sum(hidden * down, axis=1, keepdims=True), 0.0)
    prob[z] = tile
    for way in range(2):
        for two in (True, False):
            pr_copy(way, 0, two).start()

    for t in range(1, 5):
        for g in range(3):
            for way in range(2):
                if 2 * t <= last[way]:
                    ag_arrival(way, 2 * t, g).wait_recv()
            hand_on(2 * t, g)
            for way in range(2):
                if 2 * t <= last[way]:
                    pair_copy(wrap(z - sign[way] * 2 * t), g).start()
        for g in range(3):
            for way in range(2):
                ag_arrival(way, 2 * t - 1, g).wait_recv()
                pair_copy(wrap(z - sign[way] * (2 * t - 1)), g).start()
        if t == 1:
            sent_all(part.at[pl.ds(0, 7)], up_send)
            sent_all(part.at[pl.ds(0, 6)], down_send)
            sent_all(part.at[pl.ds(0, 4)], fin_send)
            sent_all(part.at[0], own_send)
            sent_all(sent.at[pl.ds(0, EXP - 1)], mine_send)
            sent_all(weights.at[pl.ds(0, 3), pl.ds(0, D_DEV)], w_send)

            @pl.when(half != core)
            def _():
                sent_all(sent, other_send)

            for way in range(2):
                pr_copy(way, 2, False).wait_recv()
                pr_copy(way, 2, False).start()
                pr_copy(way, 1, False).wait_recv()
        if t == 2:
            for way in range(2):
                pr_copy(way, 3, False).wait_recv()
            group = z // NC
            prob_out[...] = sum(prob[group * NC + c] for c in range(NC))
            pp = remote(prob_out, prob_in, pp_send, pp_recv, partner)
            pp.start()

    remote(act.at[1 - core], act.at[1 - core], pair_send, pair_recv, partner).wait_recv()

    slot_grad = jnp.zeros((ROWS, D_DEV), F32)
    for c in range(NC):
        cols = slice(c * COLS, (c + 1) * COLS)
        for i in range(3):
            full = jnp.concatenate(
                [act[h, r * NC + c, g, i].astype(F32) for h in range(2) for r in range(4) for g in range(3)],
                axis=0).astype(BF16)
            acts_ref[i, :, cols] = full
            if i < 2:
                slot_grad += dot(full, weights[i, 0:D_DEV, cols], NT)
    back_out[...] = pad_features(slot_grad).reshape(EXP, SLOT, KPAD).astype(BF16)
    for k in range(1, EXP):
        e = peer_expert(k)
        remote(back_out.at[e], back_in.at[ex], back_send, back_recv.at[ex], me, e).start()
    back_in[ex] = back_out[ex]

    pp.wait_recv()
    total = jnp.where(core == y, prob_out[...], prob_in[...])
    place = lax.broadcasted_iota(jnp.int32, (8, 128), 0) + 8 * spot
    first = 3 * (lax.rem(z, NC) * 2 + core)
    picked = [jnp.sum(jnp.where(place == first + j, total, 0.0), axis=(0, 1), keepdims=True) for j in range(3)]
    pg_ref[...] = jnp.concatenate(picked, axis=1)

    sent_all(act.at[core, pl.ds(0, 15)], ag_send)
    sent_all(act.at[core], pair_send)
    sent_all(prob.at[pl.ds(0, 6)], pr_send)
    sent_all(prob_out, pp_send)
    sent_all(back_out.at[pl.ds(0, EXP - 1)], back_send)
    for k in range(1, EXP):
        e = peer_expert(k)
        remote(back_out.at[e], back_in.at[e], back_send, back_recv.at[e], me, e).wait_recv()
    back_ref[...] = back_in[...]


def last_kernel(slots_ref, acts_ref, rows_ref, back_ref, pg_in, tg_ref, gg_ref, ug_ref, dg_ref, pg_ref, tg, grads, out_sem):
    grad_refs = (gg_ref, ug_ref, dg_ref)
    stores = [pltpu.make_async_copy(grads.at[i], grad_refs[i].at[0], out_sem.at[i]) for i in range(3)]
    stores += [pltpu.make_async_copy(tg, tg_ref, out_sem.at[3])]
    for i in range(3):
        grads[i] = dot(rows_ref[i // 2], acts_ref[i])[:D_DEV]
        stores[i].start()
    pg_ref[...] = pg_in[...]
    back_t = back_ref[...].astype(F32).reshape(ROWS, KPAD).T.astype(BF16)
    tg[...] = dot(back_t, one_hot(slots_ref))[:D_DEV].astype(BF16)
    stores[3].start()
    for copy in stores:
        copy.wait()


def local(tokens, out_grad, slot_rows, expert_counts, route_prob, w_gate, w_up, w_down):
    vmem = pl.BlockSpec(memory_space=pltpu.VMEM)
    hbm = pl.BlockSpec(memory_space=pl.ANY)
    dma = pltpu.SemaphoreType.DMA
    shape = jax.ShapeDtypeStruct
    acts, rows, back, pg = pl.pallas_call(
        kernel,
        out_shape=(
            pltpu.VMEM((3, ROWS, FF), BF16), pltpu.VMEM((2, KPAD, ROWS), BF16), pltpu.VMEM((EXP, SLOT, KPAD), BF16),
            pltpu.VMEM((1, 3), F32)),
        in_specs=[vmem] * 3 + [hbm] * 5,
        out_specs=(vmem,) * 4,
        scratch_shapes=[
            pltpu.VMEM((2, D_DEV, TOK), BF16),
            pltpu.VMEM((EXP, 2, SLOT, KPAD), BF16),
            pltpu.VMEM((EXP, 2, SLOT, KPAD), BF16),
            pltpu.VMEM((EXP, 2, SLOT, KPAD), BF16),
            pltpu.VMEM((3, 2 * KPAD, FF), BF16),
            pltpu.VMEM((Z, 9, 8, COLS), F32),
            pltpu.VMEM((8, 9, 8, COLS), F32),
            pltpu.VMEM((7, 9, 8, COLS), F32),
            pltpu.VMEM((2, 2, 9, 8, COLS), F32),
            pltpu.VMEM((9, 8, COLS), F32),
            pltpu.VMEM((2, Z, 3, 3, 8, COLS), BF16),
            pltpu.VMEM((Z, 8, 128), F32),
            pltpu.VMEM((8, 128), F32),
            pltpu.VMEM((8, 128), F32),
            pltpu.VMEM((EXP, SLOT, KPAD), BF16),
            pltpu.VMEM((EXP, SLOT, KPAD), BF16),
            dma, dma((EXP,)), dma, dma((EXP,)), dma, dma((3,)),
            dma, dma((8, 9)), dma, dma((7, 9)), dma, dma((2, 2, 9)), dma, dma((9,)),
            dma, dma((Z, 3)), dma, dma, dma, dma((Z,)), dma, dma, dma, dma((EXP,)), dma((5,)),
        ],
        compiler_params=pltpu.CompilerParams(collective_id=0, has_side_effects=True),
    )(slot_rows, route_prob, expert_counts, tokens.T, out_grad.T, w_gate[0], w_up[0], w_down[0])
    grad = shape((1, D_DEV, FF), F32)
    tg, gg, ug, dg, pg = pl.pallas_call(
        last_kernel,
        out_shape=(shape((D_DEV, TOK), BF16), grad, grad, grad, shape((1, 3), F32)),
        in_specs=[vmem] * 5,
        out_specs=(hbm,) * 4 + (vmem,),
        scratch_shapes=[pltpu.VMEM((D_DEV, TOK), BF16), pltpu.VMEM((3, D_DEV, FF), F32), dma((4,))],
    )(slot_rows, *(pltpu.with_memory_space_constraint(a, pltpu.VMEM) for a in (acts, rows, back, pg)))
    return tg.T, gg, ug, dg, pg


def solution(mesh):
    return jax.shard_map(
        local,
        mesh=mesh,
        in_specs=(
            P("expert", "fsdp"),
            P("expert", "fsdp"),
            P("expert", None, None),
            P("expert", None),
            P("expert", None),
            P("expert", "fsdp", None),
            P("expert", "fsdp", None),
            P("expert", "fsdp", None),
        ),
        out_specs=(
            P("expert", "fsdp"),
            P("expert", "fsdp", None),
            P("expert", "fsdp", None),
            P("expert", "fsdp", None),
            P("expert", "fsdp"),
        ),
        check_vma=False,
    )
```

```python
import jax
import jax.numpy as jnp
from jax import lax
from jax.experimental import pallas as pl
from jax.experimental.pallas import tpu as pltpu
from jax.sharding import PartitionSpec as P

MESH = pl.DeviceIdType.MESH
F32, BF16 = jnp.float32, jnp.bfloat16

Z = 16
EXP = 8
SLOT = 24
ROWS = EXP * SLOT
HALF = ROWS // 2
D_DEV = 80
KPAD = 128
FF = 1536
COLS = 384
NC = FF // COLS
TOK = 1024
SUB = 1
NT = (((1,), (1,)), ((), ()))


def dot(a, b, dims=(((1,), (0,)), ((), ()))):
    return lax.dot_general(a, b, dims, preferred_element_type=F32)


def slot_column(slots_ref):
    wide = jnp.concatenate([slots_ref[0].astype(F32), jnp.zeros((EXP, KPAD - SLOT), F32)], axis=1)
    tall = wide.T
    return jnp.concatenate([tall[:SLOT, e:e + 1] for e in range(EXP)], axis=0)


def one_hot(slots_ref):
    columns = lax.broadcasted_iota(jnp.int32, (ROWS, TOK), 1)
    return jnp.where(slot_column(slots_ref) == columns.astype(F32), 1.0, 0.0).astype(BF16)


def pad_features(rows):
    return jnp.concatenate([rows, jnp.zeros((ROWS, KPAD - D_DEV), F32)], axis=1)


def kernel(
    slots_ref, prob_ref, counts_ref, tok_ref, grd_ref, wg_ref, wu_ref, wd_ref,
    grads_ref, back_ref, pg_ref,
    feats, sent, mine, other, weights, part, up_in, down_in, fin_in, own_in, act, acts, rows_t,
    prob, prob_out, prob_in, back_out, back_in,
    mine_send, mine_recv, other_send, other_recv, w_send, w_recv,
    up_send, up_recv, down_send, down_recv, fin_send, fin_recv, own_send, own_recv,
    ag_send, ag_recv, pair_send, pair_recv, pr_send, pr_recv, pp_send, pp_recv, back_send, back_recv, in_sem,
):
    me = lax.axis_index("fsdp")
    ex = lax.axis_index("expert")
    core = lax.rem(me, 2)
    z = lax.rem(me // 2, Z)
    y = me // (2 * Z)
    d = 1 - 2 * core
    partner = me + d

    def at_z(pos, plane=None):
        return ((y if plane is None else plane) * Z + pos) * 2 + core

    def wrap(pos):
        return lax.rem(pos + 2 * Z, Z)

    near = [at_z(wrap(z + d)), at_z(wrap(z - d))]
    far = [at_z(wrap(z + 2 * d)), at_z(wrap(z - 2 * d))]
    cross = [at_z(wrap(z + d), 1 - y), at_z(wrap(z - d), 1 - y)]
    y_peer = at_z(z, 1 - y)
    sign = (d, -d)
    def remote(src, dst, send, recv, f, e=None):
        return pltpu.make_async_remote_copy(
            src_ref=src, dst_ref=dst, send_sem=send, recv_sem=recv,
            device_id={"fsdp": f, "expert": ex if e is None else e}, device_id_type=MESH)

    def sent_all(ref, sem):
        remote(ref, ref, sem, sem, partner).wait_send()

    barrier = pltpu.get_barrier_semaphore()
    friends = [partner, y_peer] + near + far + cross
    for k in range(1, EXP):
        e = lax.rem(ex + k, EXP)
        for f in (me, partner):
            pl.semaphore_signal(barrier, inc=1, device_id={"fsdp": f, "expert": e}, device_id_type=MESH)
    for f in friends:
        pl.semaphore_signal(barrier, inc=1, device_id={"fsdp": f, "expert": ex}, device_id_type=MESH)

    feat_in = [pltpu.make_async_copy(src, feats.at[i], in_sem.at[i]) for i, src in enumerate((tok_ref, grd_ref))]
    w_in = [
        pltpu.make_async_copy(src, weights.at[i, pl.ds(0, D_DEV)], in_sem.at[2 + i])
        for i, src in enumerate((wg_ref, wu_ref, wd_ref))]
    for copy in feat_in + w_in:
        copy.start()

    table = one_hot(slots_ref)
    for i in range(2):
        feat_in[i].wait()
        sent[:, i] = pad_features(dot(table, feats[i], NT)).reshape(EXP, SLOT, KPAD).astype(BF16)
    pad = jnp.zeros((KPAD - D_DEV, FF), BF16)
    for i in range(3):
        weights[i, D_DEV:KPAD] = pad
        weights[i, KPAD + D_DEV:2 * KPAD] = pad
        w_in[i].wait()

    pl.semaphore_wait(barrier, len(friends) + 2 * (EXP - 1))

    def peer_expert(k):
        return lax.rem(ex + k, EXP)

    half = ex // 4
    other_copies = [
        remote(sent.at[e], other.at[ex], other_send, other_recv.at[ex], partner, e)
        for e in (peer_expert(k) for k in range(EXP))]

    @pl.when(half != core)
    def _():
        for copy in other_copies:
            copy.start()

    mine_copies = [
        remote(sent.at[e], mine.at[ex], mine_send, mine_recv.at[ex], me, e)
        for e in (peer_expert(k) for k in range(1, EXP))]

    @pl.when(half == core)
    def _():
        for copy in mine_copies:
            copy.start()

    w_copies = [
        remote(weights.at[i, pl.ds(0, D_DEV)], weights.at[i, pl.ds(KPAD, D_DEV)], w_send, w_recv.at[i], partner)
        for i in range(3)]
    for copy in w_copies:
        copy.start()
    mine[ex] = sent[ex]
    for copy in w_copies:
        copy.wait_recv()

    def mine_wait(e):
        @pl.when(e != ex)
        def _():
            remote(sent.at[e], mine.at[e], mine_send, mine_recv.at[e], me, e).wait_recv()

    for k in range(4):
        e = 4 * core + k
        remote(sent.at[e], other.at[e], other_send, other_recv.at[e], partner, e).wait_recv()
        mine_wait(e)

    @pl.when(half != core)
    def _():
        for copy in mine_copies:
            copy.start()

    own_rows = [
        jnp.concatenate([
            mine[pl.ds(4 * core, 4), i].astype(F32).reshape(HALF, KPAD),
            other[pl.ds(4 * core, 4), i].astype(F32).reshape(HALF, KPAD),
        ], axis=1).astype(BF16)
        for i in range(2)
    ]
    for c in range(NC):
        for i in range(3):
            out = dot(own_rows[i // 2], weights[i, :, c * COLS:(c + 1) * COLS])
            for r in range(4):
                for g in range(3):
                    part[r * NC + c, g * 3 + i] = out[r * SLOT + g * 8:r * SLOT + g * 8 + 8]

    subs = [(q, pl.ds(q, SUB)) for q in range(0, 9, SUB)]

    def up_copy(a, q, block, src, skip=False):
        return remote(src, up_in.at[a - 1, block], up_send, up_recv.at[a - 1, q], far[0] if skip else near[0])

    def down_copy(a, q, block, src):
        return remote(src, down_in.at[a - 1, block], down_send, down_recv.at[a - 1, q], near[1])

    def fin_copy(way, other_plane, q, block, src):
        f = (cross if other_plane else near)[way]
        return remote(src, fin_in.at[way, other_plane, block], fin_send,
                      fin_recv.at[way, other_plane, q], f)

    def own_copy(q, block):
        return remote(part.at[z, block], own_in.at[block], own_send, own_recv.at[q], y_peer)

    for q, block in subs:
        up_copy(8, q, block, part.at[wrap(z + 8 * d), block], True).start()
        up_copy(7, q, block, part.at[wrap(z + 7 * d), block]).start()
        down_copy(7, q, block, part.at[wrap(z - 7 * d), block]).start()
    for q, block in subs:
        own_copy(q, block).start()

    for k in range(4):
        mine_wait(4 * (1 - core) + k)
    for i in range(2):
        rows_t[i] = mine[:, i].astype(F32).reshape(ROWS, KPAD).T.astype(BF16)

    def up_add(j, q, block):
        up_copy(j + 1, q, block, up_in.at[j, block]).wait_recv()
        up_in[j, block] = up_in[j, block] + part[wrap(z + d * j), block]

    def down_add(j, q, block):
        down_copy(j + 1, q, block, down_in.at[j, block]).wait_recv()
        down_in[j, block] = down_in[j, block] + part[wrap(z - d * j), block]

    for q, block in subs:
        down_add(6, q, block)
        down_copy(6, q, block, down_in.at[6, block]).start()
        up_copy(8, q, block, up_in.at[7, block], True).wait_recv()
        up_add(6, q, block)
        up_in[6, block] = up_in[6, block] + up_in[7, block]
        up_copy(6, q, block, up_in.at[6, block]).start()

    def ring_step(t, _):
        j = 5 - t
        for q, block in subs:
            down_add(j, q, block)
            down_copy(j, q, block, down_in.at[j, block]).start()
            up_add(j, q, block)
            up_copy(j, q, block, up_in.at[j, block]).start()
        return 0

    lax.fori_loop(0, 4, ring_step, 0)
    for q, block in subs:
        down_add(1, q, block)
        for other_plane in (1, 0):
            fin_copy(1, other_plane, q, block, down_in.at[1, block]).start()
        up_add(1, q, block)
        for other_plane in (1, 0):
            fin_copy(0, other_plane, q, block, up_in.at[1, block]).start()

    source = 4 * core + z // NC
    k8 = lax.broadcasted_iota(jnp.int32, (8, 1), 0)
    lane = lax.broadcasted_iota(jnp.int32, (8, ROWS), 1)
    count = jnp.sum(jnp.where(lax.broadcasted_iota(jnp.int32, (1, EXP), 1) == source, counts_ref[...].astype(F32), 0.0),
                    axis=1, keepdims=True)
    spot = lax.broadcasted_iota(jnp.int32, (8, 128), 1)

    def ag_copy(way, a, g, two):
        owner = wrap(z - sign[way] * a)
        return remote(act.at[core, owner, g], act.at[core, owner, g], ag_send,
                      ag_recv.at[owner, g], (far if two else near)[way])

    def ag_arrival(way, a, g):
        owner = wrap(z - sign[way] * a)
        return remote(act.at[core, owner, g], act.at[core, owner, g], ag_send, ag_recv.at[owner, g], near[way])

    def pair_copy(owner, g):
        return remote(act.at[core, owner, g], act.at[core, owner, g], pair_send, pair_recv, partner)

    def pr_copy(way, a, two):
        owner = wrap(z - sign[way] * a)
        return remote(prob.at[owner], prob.at[owner], pr_send, pr_recv.at[owner],
                      (far if two else near)[way])

    last = (8, 7)

    def hand_on(a, g):
        for two in (True, False):
            for way in range(2):
                if a + (2 if two else 1) <= last[way]:
                    ag_copy(way, a, g, two).start()

    tile = jnp.zeros((8, 128), F32)
    for g in range(3):
        sums = []
        for i in range(3):
            q = (g * 3 + i) // SUB * SUB
            block = pl.ds(q, SUB)
            if (g * 3 + i) % SUB == 0:
                own_copy(q, block).wait_recv()
                for way in range(2):
                    for other_plane in range(2):
                        fin_copy(way, other_plane, q, block, fin_in.at[way, other_plane, block]).wait_recv()
            n = g * 3 + i
            here = (fin_in[0, 0, n] + fin_in[1, 0, n]) + part[z, n]
            there = (fin_in[0, 1, n] + fin_in[1, 1, n]) + own_in[n]
            sums.append(here + there)
        gate, up, down = sums
        slot = k8 + 8 * g
        live = (slot.astype(F32) < count).astype(F32)
        scale = live * jnp.sum(jnp.where(lane == slot + SLOT * source, prob_ref[...], 0.0), axis=1, keepdims=True)
        sigmoid = jax.nn.sigmoid(gate)
        silu = gate * sigmoid
        hidden = (silu * up).astype(BF16).astype(F32)
        hidden_grad = down * scale
        act[core, z, g, 0] = (hidden_grad * up * sigmoid * (1.0 + gate * (1.0 - sigmoid))).astype(BF16)
        act[core, z, g, 1] = (hidden_grad * silu).astype(BF16)
        act[core, z, g, 2] = (hidden * scale).astype(BF16)
        hand_on(0, g)
        pair_copy(z, g).start()
        tile += jnp.where(spot == g, live * jnp.sum(hidden * down, axis=1, keepdims=True), 0.0)
    prob[z] = tile
    for way in range(2):
        for two in (True, False):
            pr_copy(way, 0, two).start()

    for t in range(1, 5):
        for g in range(3):
            for way in range(2):
                if 2 * t <= last[way]:
                    ag_arrival(way, 2 * t, g).wait_recv()
            hand_on(2 * t, g)
            for way in range(2):
                if 2 * t <= last[way]:
                    pair_copy(wrap(z - sign[way] * 2 * t), g).start()
        for g in range(3):
            for way in range(2):
                ag_arrival(way, 2 * t - 1, g).wait_recv()
                pair_copy(wrap(z - sign[way] * (2 * t - 1)), g).start()
        if t == 1:
            sent_all(part.at[pl.ds(0, 7)], up_send)
            sent_all(part.at[pl.ds(0, 6)], down_send)
            sent_all(part.at[pl.ds(0, 4)], fin_send)
            sent_all(part.at[0], own_send)
            sent_all(sent.at[pl.ds(0, EXP - 1)], mine_send)
            sent_all(weights.at[pl.ds(0, 3), pl.ds(0, D_DEV)], w_send)

            @pl.when(half != core)
            def _():
                sent_all(sent, other_send)

            for way in range(2):
                pr_copy(way, 2, False).wait_recv()
                pr_copy(way, 2, False).start()
                pr_copy(way, 1, False).wait_recv()
        if t == 2:
            for way in range(2):
                pr_copy(way, 3, False).wait_recv()
            group = z // NC
            prob_out[...] = sum(prob[group * NC + c] for c in range(NC))
            pp = remote(prob_out, prob_in, pp_send, pp_recv, partner)
            pp.start()

    remote(act.at[1 - core], act.at[1 - core], pair_send, pair_recv, partner).wait_recv()

    slot_grad = jnp.zeros((ROWS, D_DEV), F32)
    for c in range(NC):
        cols = slice(c * COLS, (c + 1) * COLS)
        for i in range(3):
            full = jnp.concatenate(
                [act[h, r * NC + c, g, i].astype(F32) for h in range(2) for r in range(4) for g in range(3)],
                axis=0).astype(BF16)
            acts[i, :, cols] = full
            if i < 2:
                slot_grad += dot(full, weights[i, 0:D_DEV, cols], NT)
    back_out[...] = pad_features(slot_grad).reshape(EXP, SLOT, KPAD).astype(BF16)
    for k in range(1, EXP):
        e = peer_expert(k)
        remote(back_out.at[e], back_in.at[ex], back_send, back_recv.at[ex], me, e).start()
    back_in[ex] = back_out[ex]

    for i in range(3):
        grads_ref[i] = dot(rows_t[i // 2], acts[i])[:D_DEV]

    pp.wait_recv()
    total = jnp.where(core == y, prob_out[...], prob_in[...])
    place = lax.broadcasted_iota(jnp.int32, (8, 128), 0) + 8 * spot
    first = 3 * (lax.rem(z, NC) * 2 + core)
    picked = [jnp.sum(jnp.where(place == first + j, total, 0.0), axis=(0, 1), keepdims=True) for j in range(3)]
    pg_ref[...] = jnp.concatenate(picked, axis=1)

    sent_all(act.at[core, pl.ds(0, 15)], ag_send)
    sent_all(act.at[core], pair_send)
    sent_all(prob.at[pl.ds(0, 6)], pr_send)
    sent_all(prob_out, pp_send)
    sent_all(back_out.at[pl.ds(0, EXP - 1)], back_send)
    for k in range(1, EXP):
        e = peer_expert(k)
        remote(back_out.at[e], back_in.at[e], back_send, back_recv.at[e], me, e).wait_recv()
    back_ref[...] = back_in[...]


def last_kernel(slots_ref, grads, back_ref, pg_in, tg_ref, gg_ref, ug_ref, dg_ref, pg_ref, tg, out_sem):
    stores = [pltpu.make_async_copy(grads.at[i], out.at[0], out_sem.at[i]) for i, out in enumerate((gg_ref, ug_ref, dg_ref))]
    stores += [pltpu.make_async_copy(tg, tg_ref, out_sem.at[3])]
    for i in range(3):
        stores[i].start()
    pg_ref[...] = pg_in[...]
    back_t = back_ref[...].astype(F32).reshape(ROWS, KPAD).T.astype(BF16)
    tg[...] = dot(back_t, one_hot(slots_ref))[:D_DEV].astype(BF16)
    stores[3].start()
    for copy in stores:
        copy.wait()


def local(tokens, out_grad, slot_rows, expert_counts, route_prob, w_gate, w_up, w_down):
    vmem = pl.BlockSpec(memory_space=pltpu.VMEM)
    hbm = pl.BlockSpec(memory_space=pl.ANY)
    dma = pltpu.SemaphoreType.DMA
    shape = jax.ShapeDtypeStruct
    grads, back, pg = pl.pallas_call(
        kernel,
        out_shape=(
            pltpu.VMEM((3, D_DEV, FF), F32), pltpu.VMEM((EXP, SLOT, KPAD), BF16), pltpu.VMEM((1, 3), F32)),
        in_specs=[vmem] * 3 + [hbm] * 5,
        out_specs=(vmem,) * 3,
        scratch_shapes=[
            pltpu.VMEM((2, D_DEV, TOK), BF16),
            pltpu.VMEM((EXP, 2, SLOT, KPAD), BF16),
            pltpu.VMEM((EXP, 2, SLOT, KPAD), BF16),
            pltpu.VMEM((EXP, 2, SLOT, KPAD), BF16),
            pltpu.VMEM((3, 2 * KPAD, FF), BF16),
            pltpu.VMEM((Z, 9, 8, COLS), F32),
            pltpu.VMEM((8, 9, 8, COLS), F32),
            pltpu.VMEM((7, 9, 8, COLS), F32),
            pltpu.VMEM((2, 2, 9, 8, COLS), F32),
            pltpu.VMEM((9, 8, COLS), F32),
            pltpu.VMEM((2, Z, 3, 3, 8, COLS), BF16),
            pltpu.VMEM((3, ROWS, FF), BF16),
            pltpu.VMEM((2, KPAD, ROWS), BF16),
            pltpu.VMEM((Z, 8, 128), F32),
            pltpu.VMEM((8, 128), F32),
            pltpu.VMEM((8, 128), F32),
            pltpu.VMEM((EXP, SLOT, KPAD), BF16),
            pltpu.VMEM((EXP, SLOT, KPAD), BF16),
            dma, dma((EXP,)), dma, dma((EXP,)), dma, dma((3,)),
            dma, dma((8, 9)), dma, dma((7, 9)), dma, dma((2, 2, 9)), dma, dma((9,)),
            dma, dma((Z, 3)), dma, dma, dma, dma((Z,)), dma, dma, dma, dma((EXP,)), dma((5,)),
        ],
        compiler_params=pltpu.CompilerParams(collective_id=0, has_side_effects=True),
    )(slot_rows, route_prob, expert_counts, tokens.T, out_grad.T, w_gate[0], w_up[0], w_down[0])
    grad = shape((1, D_DEV, FF), F32)
    tg, gg, ug, dg, pg = pl.pallas_call(
        last_kernel,
        out_shape=(shape((D_DEV, TOK), BF16), grad, grad, grad, shape((1, 3), F32)),
        in_specs=[vmem] * 4,
        out_specs=(hbm,) * 4 + (vmem,),
        scratch_shapes=[pltpu.VMEM((D_DEV, TOK), BF16), dma((4,))],
    )(slot_rows, *(pltpu.with_memory_space_constraint(a, pltpu.VMEM) for a in (grads, back, pg)))
    return tg.T, gg, ug, dg, pg


def solution(mesh):
    return jax.shard_map(
        local,
        mesh=mesh,
        in_specs=(
            P("expert", "fsdp"),
            P("expert", "fsdp"),
            P("expert", None, None),
            P("expert", None),
            P("expert", None),
            P("expert", "fsdp", None),
            P("expert", "fsdp", None),
            P("expert", "fsdp", None),
        ),
        out_specs=(
            P("expert", "fsdp"),
            P("expert", "fsdp", None),
            P("expert", "fsdp", None),
            P("expert", "fsdp", None),
            P("expert", "fsdp"),
        ),
        check_vma=False,
    )
```
